128 devices in a mesh: pos: 64 (over z, y, x), head: 2 (over core).
Axes of the slice: x: 4, y: 4, z: 4, core: 2. Of those that a mesh axis runs over, the one named last changes fastest.
Arguments:
- inputs: bfloat16 [65536, 1024], P('pos'), may hold values from -400 to 400
- valid_blocks: int32 [512], P('pos'), may hold values from 0 to 1, as said below
- latents: bfloat16 [2048, 1024], P('pos'), may hold values from -6 to 6
- w_query: bfloat16 [1024, 1024], P(None, 'head'), may hold values from -0.1875 to 0.1875
- w_key: bfloat16 [1024, 1024], P(None, 'head'), may hold values from -0.1875 to 0.1875
- w_value: bfloat16 [1024, 1024], P(None, 'head'), may hold values from -0.1875 to 0.1875
- w_out: bfloat16 [1024, 1024], P('head'), may hold values from -0.1875 to 0.1875
- w_mlp: bfloat16 [1024, 1024], replicated, may hold values from -0.1875 to 0.1875
- w_lkey: bfloat16 [1024, 1024], P(None, 'head'), may hold values from -0.1875 to 0.1875
- w_lvalue: bfloat16 [1024, 1024], P(None, 'head'), may hold values from -0.1875 to 0.1875
- w_pquery: bfloat16 [1024, 1024], P(None, 'head'), may hold values from -0.1875 to 0.1875
- w_pout: bfloat16 [1024, 1024], P('head'), may hold values from -0.1875 to 0.1875
Outputs:
- decoded: bfloat16 [65536, 1024], P(('pos', 'head'))
The draws below stay inside these ranges and needn't reach their ends.
Inputs may be any that keep to these rules, and one draw needn't show every extreme that they name: `valid_blocks`: within the 1024 positions of each device the blocks marked 1 come first; every device has at least one block marked 1, and some device has all its blocks marked 1.
All inputs are finite; a program needn't handle non-finite values.
Results may differ from the reference program's by a relative error of at most 0.017.
The reference program's roundings to bfloat16 on the way count: a program that leaves them out, or rounds other values in their place, can miss the bound.
Values may be sent and summed in bfloat16 or wider, within the bound.
No kernel may reach another device: no remote copies, remote signals or barrier semaphores. Data moves between devices by JAX's collectives and lax.ppermute only.
A program may use at most 128 MiB of HBM per device.

```python
import jax
import jax.numpy as jnp
from jax import lax

D = 1024
HEADS = 8
HEAD_DIM = 128
LAT = 2048
POS_DEV = 1024
BLK = 128
INNER = 1024
N_POS = 64


def draw_inputs(key, part):
    key_base = jax.random.fold_in(key, 11)
    normal_part = jax.random.truncated_normal(key_base, -6.0, 6.0, (POS_DEV * N_POS, D), jnp.float32)
    return normal_part.astype(jnp.bfloat16)


def draw_valid_blocks(key, part):
    blocks_each = POS_DEV // BLK
    key_counts = jax.random.fold_in(key, 21)
    key_full = jax.random.fold_in(key, 22)
    counts = jax.random.randint(key_counts, (N_POS,), 1, blocks_each + 1)
    fullest = jax.random.randint(key_full, (), 0, N_POS)
    counts = jnp.where(jnp.arange(N_POS) == fullest, blocks_each, counts)
    marks = jnp.arange(blocks_each)[None, :] < counts[:, None]
    return marks.astype(jnp.int32).reshape(N_POS * blocks_each)


def shard_levels(key, shape, split, least, high):
    def one(dim, shards_of):
        heights = jax.random.uniform(jax.random.fold_in(jax.random.fold_in(key, 6), dim), (shards_of,), jnp.float32, least / len(split), high / len(split))
        return jnp.repeat(jnp.exp(heights), shape[dim] // shards_of).reshape((-1,) + (1,) * (len(shape) - dim - 1))

    loudness = one(*split[0])
    for cut in split[1:]:
        loudness = loudness * one(*cut)
    return loudness


def scatter_about(key, extent, spread, most, pieces=(), held_as=jnp.bfloat16):
    loudness = shard_levels(key, extent, pieces, -0.22, 0.18) if pieces else 1.0
    result = jax.random.normal(key, extent, jnp.float32) * spread * loudness
    return jnp.minimum(jnp.maximum(result, -most), most).astype(held_as)


def setup_inputs(seed: int = 0) -> dict:
    key_of = jax.random.split(jax.random.key(seed), 13)
    inputs = draw_inputs(jax.random.fold_in(key_of[12], 71), 0)
    valid_blocks = draw_valid_blocks(jax.random.fold_in(key_of[12], 71), 0)
    latents = scatter_about(key_of[2], (LAT, D), 1.0, 6.0, ((0, 64),))
    w_query = scatter_about(key_of[3], (D, INNER), D ** -0.5, 0.1875, ((1, 2),))
    w_key = scatter_about(key_of[4], (D, INNER), D ** -0.5, 0.1875, ((1, 2),))
    w_value = scatter_about(key_of[5], (D, INNER), D ** -0.5, 0.1875, ((1, 2),))
    w_out = scatter_about(key_of[6], (INNER, D), INNER ** -0.5, 0.1875, ((0, 2),))
    w_mlp = scatter_about(key_of[7], (D, D), D ** -0.5, 0.1875)
    w_lkey = scatter_about(key_of[8], (D, INNER), D ** -0.5, 0.1875, ((1, 2),))
    w_lvalue = scatter_about(key_of[9], (D, INNER), D ** -0.5, 0.1875, ((1, 2),))
    w_pquery = scatter_about(key_of[10], (D, INNER), D ** -0.5, 0.1875, ((1, 2),))
    w_pout = scatter_about(key_of[11], (INNER, D), INNER ** -0.5, 0.1875, ((0, 2),))
    return {"inputs": inputs, "valid_blocks": valid_blocks, "latents": latents, "w_query": w_query, "w_key": w_key, "w_value": w_value, "w_out": w_out, "w_mlp": w_mlp, "w_lkey": w_lkey, "w_lvalue": w_lvalue, "w_pquery": w_pquery, "w_pout": w_pout}


masked_score = -1e+30
epsilon = 1e-05

def rms_norm(values):
    return values * lax.rsqrt(lax.optimization_barrier(jnp.mean(values * values, axis=-1, keepdims=True)) + epsilon)

def widen(values):
    return lax.optimization_barrier(values).astype(jnp.float32)

def reference(inputs, valid_blocks, latents, w_query, w_key, w_value, w_out, w_mlp, w_lkey, w_lvalue, w_pquery, w_pout):
    scaling = HEAD_DIM ** (-0.5)
    positions = inputs.shape[0]
    inner = HEADS * HEAD_DIM
    pos_keys = widen(jnp.dot(inputs, w_key, preferred_element_type=jnp.float32).astype(jnp.bfloat16)).reshape(positions, HEADS, HEAD_DIM)
    pos_values = widen(jnp.dot(inputs, w_value, preferred_element_type=jnp.float32).astype(jnp.bfloat16)).reshape(positions, HEADS, HEAD_DIM)
    alive_mask = jnp.repeat(valid_blocks, BLK) > 0
    lat_block = min(LAT, 128)
    lat_queries = widen(jnp.dot(latents, w_query, preferred_element_type=jnp.float32).astype(jnp.bfloat16))
    lat_queries = lat_queries.reshape(LAT // lat_block, lat_block, HEADS, HEAD_DIM)

    def cross_block(query_rows):
        scores = jnp.einsum('lhe,phe->lhp', query_rows, pos_keys) * scaling
        scores = jnp.where(alive_mask[None, None, :], scores, masked_score)
        row_max = lax.optimization_barrier(jnp.max(scores, axis=-1, keepdims=True))
        exponent = jnp.exp(scores - row_max)
        totals = lax.optimization_barrier(jnp.sum(exponent, axis=-1))
        weights = widen(exponent.astype(jnp.bfloat16))
        numerators = jnp.einsum('lhp,phe->lhe', weights, pos_values)
        return (numerators / totals[..., None]).astype(jnp.bfloat16).reshape(lat_block, inner)
    attended = lax.map(cross_block, lat_queries).reshape(LAT, inner)
    merged = jnp.dot(attended, w_out, preferred_element_type=jnp.float32)
    normed = rms_norm(merged)
    hidden = jax.nn.gelu(jnp.dot(normed.astype(jnp.bfloat16), w_mlp, preferred_element_type=jnp.float32))
    lat_rows = (normed + hidden).astype(jnp.bfloat16)
    lat_keys = widen(jnp.dot(lat_rows, w_lkey, preferred_element_type=jnp.float32).astype(jnp.bfloat16)).reshape(LAT, HEADS, HEAD_DIM)
    lat_values = widen(jnp.dot(lat_rows, w_lvalue, preferred_element_type=jnp.float32).astype(jnp.bfloat16)).reshape(LAT, HEADS, HEAD_DIM)
    pos_block = min(positions, 512)
    pos_queries = widen(jnp.dot(inputs, w_pquery, preferred_element_type=jnp.float32).astype(jnp.bfloat16))
    pos_queries = pos_queries.reshape(positions // pos_block, pos_block, HEADS, HEAD_DIM)

    def decode_block(query_rows):
        scores = jnp.einsum('phe,lhe->phl', query_rows, lat_keys) * scaling
        row_max = lax.optimization_barrier(jnp.max(scores, axis=-1, keepdims=True))
        exponent = jnp.exp(scores - row_max)
        totals = lax.optimization_barrier(jnp.sum(exponent, axis=-1))
        weights = widen(exponent.astype(jnp.bfloat16))
        numerators = jnp.einsum('phl,lhe->phe', weights, lat_values)
        return (numerators / totals[..., None]).astype(jnp.bfloat16).reshape(pos_block, inner)
    pos_attended = lax.map(decode_block, pos_queries).reshape(positions, inner)
    final = jnp.dot(pos_attended, w_pout, preferred_element_type=jnp.float32)
    return rms_norm(final).astype(jnp.bfloat16)
```

```python
import functools

import jax
import jax.numpy as jnp
from jax import lax
from jax.experimental import pallas as pl
from jax.experimental.pallas import tpu as pltpu
from jax.sharding import PartitionSpec as P

HEAD_DIM = 128
BLK = 128
SCALE = HEAD_DIM ** (-0.5)
LOG2E = 1.4426950408889634
MASKED = -1e30
EPS = 1e-05
F32 = jnp.float32
BF16 = jnp.bfloat16
ROW_BLOCK = 256
LSE_ROWS = 8


def rms_norm(values):
    return values * lax.rsqrt(jnp.mean(values * values, axis=-1, keepdims=True) + EPS)


def nt_dot(a, b):
    return lax.dot_general(a, b, (((1,), (1,)), ((), ())), preferred_element_type=F32)


def cross_kernel(count_ref, q_ref, k_ref, v_ref, out_ref, *, lat_local):
    heads = q_ref.shape[1] // HEAD_DIM
    rows = q_ref.shape[0]
    owners = rows // lat_local
    span = heads * lat_local
    keys = k_ref.shape[0]
    valid = count_ref[0] * BLK

    def run(masked):
        columns = []
        for h in range(heads):
            cols = slice(h * HEAD_DIM, (h + 1) * HEAD_DIM)
            s = nt_dot(q_ref[:, cols], k_ref[:, cols])
            if masked:
                where = lax.broadcasted_iota(jnp.int32, s.shape, 1) < valid
                s = jnp.where(where, s, MASKED)
            m = jnp.max(s, axis=1, keepdims=True)
            p = jnp.exp2((s - m) * (SCALE * LOG2E))
            total = jnp.sum(p, axis=1, keepdims=True)
            o = jnp.dot(p.astype(BF16), v_ref[:, cols], preferred_element_type=F32)
            o = (o / total).astype(BF16)
            out_ref[:, h * lat_local : (h + 1) * lat_local, :] = o.reshape(owners, lat_local, HEAD_DIM)
            columns.append(m * SCALE + jnp.log(total))
        for d in range(owners):
            part = jnp.concatenate(
                [c[d * lat_local : (d + 1) * lat_local] for c in columns], axis=0
            )
            row = jnp.transpose(jnp.broadcast_to(part, (span, HEAD_DIM)))[:LSE_ROWS]
            hi = row.astype(BF16).astype(F32)
            mid = (row - hi).astype(BF16).astype(F32)
            low = (row - hi - mid).astype(BF16).astype(F32)
            place = lax.broadcasted_iota(jnp.int32, row.shape, 0)
            packed = jnp.where(place == 0, hi, jnp.where(place == 1, mid, jnp.where(place == 2, low, 0.0)))
            out_ref[d, span : span + LSE_ROWS, :] = packed.astype(BF16)

    full = valid == keys

    @pl.when(full)
    def _():
        run(False)

    @pl.when(jnp.logical_not(full))
    def _():
        run(True)


def combine_kernel(core_ref, r_ref, w_ref, own_ref, other_ref, terms_ref, *, lat_local):
    devices, tall, _ = r_ref.shape
    span = tall - LSE_ROWS
    heads = span // lat_local
    lse = jnp.sum(r_ref[:, span : span + LSE_ROWS, :].astype(F32), axis=1)
    w = jnp.exp(lse - jnp.max(lse, axis=0, keepdims=True))
    w = w / jnp.sum(w, axis=0, keepdims=True)
    wt = jnp.transpose(w)
    acc = jnp.zeros((span, HEAD_DIM), F32)
    for d in range(devices):
        acc = acc + wt[:, d : d + 1] * r_ref[d, :span, :].astype(F32)
    attended = acc.astype(BF16)
    terms = jnp.zeros((lat_local, w_ref.shape[1]), F32)
    for h in range(heads):
        terms = terms + jnp.dot(
            attended[h * lat_local : (h + 1) * lat_local],
            w_ref[h * HEAD_DIM : (h + 1) * HEAD_DIM, :],
            preferred_element_type=F32,
        )
    half = lat_local // 2
    terms_ref[...] = terms.reshape(2, half, w_ref.shape[1])
    own_ref[...] = terms_ref[core_ref[0]]
    other_ref[...] = terms_ref[1 - core_ref[0]].astype(BF16)


def latent_kernel(own_ref, recv_ref, w_ref, out_ref):
    normed = rms_norm(own_ref[...] + recv_ref[...].astype(F32))
    hidden = jax.nn.gelu(jnp.dot(normed.astype(BF16), w_ref[...], preferred_element_type=F32))
    rows = (normed + hidden).astype(BF16)
    out_ref[...] = jnp.broadcast_to(rows[None], out_ref.shape)


def decode_kernel(base_ref, q_ref, ka_ref, va_ref, kb_ref, vb_ref, w_ref, out_ref):
    heads = q_ref.shape[1] // HEAD_DIM
    outs = []
    for h in range(heads):
        cols = slice(h * HEAD_DIM, (h + 1) * HEAD_DIM)
        q = q_ref[:, cols]
        sa = nt_dot(q, ka_ref[:, cols])
        sb = nt_dot(q, kb_ref[:, cols])
        m = jnp.maximum(jnp.max(sa, axis=1, keepdims=True), jnp.max(sb, axis=1, keepdims=True))
        pa = jnp.exp2((sa - m) * (SCALE * LOG2E))
        pb = jnp.exp2((sb - m) * (SCALE * LOG2E))
        total = jnp.sum(pa, axis=1, keepdims=True) + jnp.sum(pb, axis=1, keepdims=True)
        o = jnp.dot(pa.astype(BF16), va_ref[:, cols], preferred_element_type=F32)
        o = o + jnp.dot(pb.astype(BF16), vb_ref[:, cols], preferred_element_type=F32)
        outs.append((o / total).astype(BF16))
    attended = jnp.concatenate(outs, axis=1)
    out_ref[...] = jnp.dot(attended, w_ref[...], preferred_element_type=F32).astype(out_ref.dtype)


def final_kernel(own_ref, recv_ref, out_ref):
    out_ref[...] = rms_norm(own_ref[...] + recv_ref[...].astype(F32)).astype(out_ref.dtype)


def full_spec(array):
    return pl.BlockSpec(array.shape, lambda *_: (0,) * array.ndim)


def params(limit=56 << 20):
    return pltpu.CompilerParams(vmem_limit_bytes=limit)


def cross(count, q, k, v, lat_local):
    lat, columns = q.shape
    heads = columns // HEAD_DIM
    tall = heads * lat_local + LSE_ROWS
    block = min(ROW_BLOCK, lat)
    return pl.pallas_call(
        functools.partial(cross_kernel, lat_local=lat_local),
        out_shape=jax.ShapeDtypeStruct((lat // lat_local, tall, HEAD_DIM), BF16),
        grid_spec=pltpu.PrefetchScalarGridSpec(
            num_scalar_prefetch=1,
            grid=(lat // block,),
            in_specs=[
                pl.BlockSpec((block, columns), lambda i, c: (i, 0)),
                full_spec(k),
                full_spec(v),
            ],
            out_specs=pl.BlockSpec((block // lat_local, tall, HEAD_DIM), lambda i, c: (i, 0, 0)),
        ),
        compiler_params=params(),
        name="cross",
    )(count, q, k, v)


def combine(core, r, w_out, lat_local):
    width = w_out.shape[1]
    half = lat_local // 2
    vmem = pl.BlockSpec(memory_space=pltpu.VMEM)
    return pl.pallas_call(
        functools.partial(combine_kernel, lat_local=lat_local),
        out_shape=(
            jax.ShapeDtypeStruct((half, width), F32),
            jax.ShapeDtypeStruct((half, width), BF16),
        ),
        in_specs=[pl.BlockSpec(memory_space=pltpu.SMEM), vmem, vmem],
        out_specs=(vmem, vmem),
        scratch_shapes=[pltpu.VMEM((2, half, width), F32)],
        compiler_params=params(24 << 20),
        name="combine",
    )(core, r, w_out)


def latent_rows(own, recv, w_mlp, devices):
    vmem = pl.BlockSpec(memory_space=pltpu.VMEM)
    return pl.pallas_call(
        latent_kernel,
        out_shape=jax.ShapeDtypeStruct((devices,) + own.shape, BF16),
        in_specs=[vmem] * 3,
        out_specs=vmem,
        compiler_params=params(24 << 20),
        name="latent",
    )(own, recv, w_mlp)


def decode(base, q, ka, va, kb, vb, w_pout, dtype):
    rows, columns = q.shape[0] // 2, q.shape[1]
    width = w_pout.shape[1]
    block = min(ROW_BLOCK, rows)
    return pl.pallas_call(
        decode_kernel,
        out_shape=jax.ShapeDtypeStruct((rows, width), dtype),
        grid_spec=pltpu.PrefetchScalarGridSpec(
            num_scalar_prefetch=1,
            grid=(rows // block,),
            in_specs=[
                pl.BlockSpec((block, columns), lambda i, b: (b[0] * (rows // block) + i, 0)),
                *[full_spec(x) for x in (ka, va, kb, vb, w_pout)],
            ],
            out_specs=pl.BlockSpec((block, width), lambda i, b: (i, 0)),
        ),
        compiler_params=params(),
        cost_estimate=pl.CostEstimate(
            flops=4 * rows * columns * 2 * ka.shape[0], bytes_accessed=8 << 20, transcendentals=1 << 22
        ),
        name="decode",
    )(base, q, ka, va, kb, vb, w_pout)


def finish(own, recv):
    rows, width = own.shape
    block = min(256, rows)
    spec = pl.BlockSpec((block, width), lambda i: (i, 0))
    return pl.pallas_call(
        final_kernel,
        out_shape=jax.ShapeDtypeStruct((rows, width), BF16),
        grid=(rows // block,),
        in_specs=[spec, spec],
        out_specs=spec,
        compiler_params=params(24 << 20),
        name="finish",
    )(own, recv)


def project(a, w):
    return jnp.dot(a, w, preferred_element_type=F32).astype(BF16)


def per_device(
    devices,
    inputs,
    valid_blocks,
    latents,
    w_query,
    w_key,
    w_value,
    w_out,
    w_mlp,
    w_lkey,
    w_lvalue,
    w_pquery,
    w_pout,
):
    lat_local = latents.shape[0]
    columns = w_key.shape[1]
    width = inputs.shape[1]
    core = lax.axis_index("head").astype(jnp.int32).reshape(1)
    swap = [(0, 1), (1, 0)]

    own_queries = project(latents, w_query)
    spread = jnp.broadcast_to(own_queries[None], (devices,) + own_queries.shape)
    lat_queries = lax.all_to_all(spread, "pos", 0, 0).reshape(devices * lat_local, columns)
    keys = project(inputs, w_key)
    values = project(inputs, w_value)
    pos_queries = project(inputs, w_pquery)

    count = jnp.sum(valid_blocks).astype(jnp.int32).reshape(1)
    partial = cross(count, lat_queries, keys, values, lat_local)
    gathered = lax.all_to_all(partial, "pos", 0, 0)
    own, other = combine(core, gathered, w_out, lat_local)
    recv = lax.ppermute(other, "head", swap)
    rows = latent_rows(own, recv, w_mlp, devices)
    rows_a = lax.all_to_all(rows, "pos", 0, 0).reshape(devices * lat_local // 2, width)
    rows_b = lax.ppermute(rows_a, "head", swap)
    ka, va = project(rows_a, w_lkey), project(rows_a, w_lvalue)
    kb, vb = project(rows_b, w_lkey), project(rows_b, w_lvalue)
    away = decode(1 - core, pos_queries, ka, va, kb, vb, w_pout, BF16)
    arrived = lax.ppermute(away, "head", swap)
    home = decode(core, pos_queries, ka, va, kb, vb, w_pout, F32)
    return finish(home, arrived)


def solution(mesh):
    placed = (
        P("pos", None),
        P("pos"),
        P("pos", None),
        P(None, "head"),
        P(None, "head"),
        P(None, "head"),
        P("head", None),
        P(),
        P(None, "head"),
        P(None, "head"),
        P(None, "head"),
        P("head", None),
    )
    return jax.shard_map(
        functools.partial(per_device, mesh.shape["pos"]),
        mesh=mesh,
        in_specs=placed,
        out_specs=P(("pos", "head"), None),
        check_vma=False,
    )
```

```python
import functools

import jax
import jax.numpy as jnp
from jax import lax
from jax.experimental import pallas as pl
from jax.experimental.pallas import tpu as pltpu
from jax.sharding import PartitionSpec as P


HEAD_DIM = 128
BLK = 128
SCALE = HEAD_DIM ** (-0.5)
LOG2E = 1.4426950408889634
MASKED = -1e30
EPS = 1e-05
F32 = jnp.float32
BF16 = jnp.bfloat16
ROW_BLOCK = 256
LSE_ROWS = 8


AXES = ("pos", "head")
SIDE = 4
ORDER = (1, 3, 2)


def plane_groups():
    def device(z, y, x, core):
        return ((z * SIDE + y) * SIDE + x) * 2 + core

    r = range(SIDE)
    plane = [[device(z, y, x, 0) for y in r for x in r] for z in r]
    plane += [[device(z, y, x, 1) for z in r for x in r] for y in r]
    long = {}
    for s in range(1, SIDE):
        long[s] = [
            pair
            for z in r
            for y in r
            for x in r
            for pair in (
                (device(z, y, x, 0), device((z + s) % SIDE, y, x, 0)),
                (device(z, y, x, 1), device(z, (y + s) % SIDE, x, 1)),
            )
        ]
    return plane, long


def rms_norm(values):
    return values * lax.rsqrt(jnp.mean(values * values, axis=-1, keepdims=True) + EPS)


def nt_dot(a, b):
    return lax.dot_general(a, b, (((1,), (1,)), ((), ())), preferred_element_type=F32)


def pieces(row):
    hi = row.astype(BF16).astype(F32)
    mid = (row - hi).astype(BF16).astype(F32)
    low = (row - hi - mid).astype(BF16).astype(F32)
    place = lax.broadcasted_iota(jnp.int32, row.shape, 0)
    packed = jnp.where(place == 0, hi, jnp.where(place == 1, mid, jnp.where(place == 2, low, 0.0)))
    return packed.astype(BF16)


def cross_kernel(count_ref, q_ref, k_ref, v_ref, out_ref, *, lat_local):
    heads = q_ref.shape[1] // HEAD_DIM
    rows = q_ref.shape[0]
    owners = rows // lat_local
    span = heads * lat_local
    keys = k_ref.shape[0]
    valid = count_ref[0] * BLK

    live = lax.broadcasted_iota(jnp.int32, (1, keys), 1) < valid
    bias = jnp.where(live, 0.0, MASKED)
    columns = []
    for h in range(heads):
        cols = slice(h * HEAD_DIM, (h + 1) * HEAD_DIM)
        s = nt_dot(q_ref[:, cols], k_ref[:, cols]) + bias
        m = jnp.max(s, axis=1, keepdims=True)
        p = jnp.exp2((s - m) * (SCALE * LOG2E))
        total = jnp.sum(p, axis=1, keepdims=True)
        o = jnp.dot(p.astype(BF16), v_ref[:, cols], preferred_element_type=F32)
        o = (o / total).astype(BF16)
        out_ref[:, h * lat_local : (h + 1) * lat_local, :] = o.reshape(owners, lat_local, HEAD_DIM)
        columns.append(m * SCALE + jnp.log(total))
    for d in range(owners):
        part = jnp.concatenate([c[d * lat_local : (d + 1) * lat_local] for c in columns], axis=0)
        row = jnp.transpose(jnp.broadcast_to(part, (span, HEAD_DIM)))[:LSE_ROWS]
        out_ref[d, span : span + LSE_ROWS, :] = pieces(row)


def join_kernel(*refs):
    *parts, out_ref = refs
    owners, tall, _ = out_ref.shape
    span = tall - LSE_ROWS
    lses = [jnp.sum(r[:, span : span + LSE_ROWS, :].astype(F32), axis=1) for r in parts]
    top = functools.reduce(jnp.maximum, lses)
    ws = [jnp.exp(x - top) for x in lses]
    total = functools.reduce(jnp.add, ws)
    lse = top + jnp.log(total)
    wts = [jnp.transpose(w / total) for w in ws]
    for d in range(owners):
        acc = jnp.zeros((span, HEAD_DIM), F32)
        for wt, r in zip(wts, parts):
            acc = acc + wt[:, d : d + 1] * r[d, :span, :].astype(F32)
        out_ref[d, :span, :] = acc.astype(BF16)
        row = jnp.broadcast_to(lse[d : d + 1, :], (LSE_ROWS, HEAD_DIM))
        out_ref[d, span : span + LSE_ROWS, :] = pieces(row)


def combine_kernel(core_ref, *refs, lat_local):
    *parts, w_ref, own_ref, other_ref, terms_ref = refs
    terms = jnp.zeros((lat_local, w_ref.shape[1]), F32)
    first = 0
    for r_ref in parts:
        devices, tall, _ = r_ref.shape
        span = tall - LSE_ROWS
        lse = jnp.sum(r_ref[:, span : span + LSE_ROWS, :].astype(F32), axis=1)
        w = jnp.exp(lse - jnp.max(lse, axis=0, keepdims=True))
        w = w / jnp.sum(w, axis=0, keepdims=True)
        wt = jnp.transpose(w)
        acc = jnp.zeros((span, HEAD_DIM), F32)
        for d in range(devices):
            acc = acc + wt[:span, d : d + 1] * r_ref[d, :span, :].astype(F32)
        attended = acc.astype(BF16)
        for h in range(span // lat_local):
            terms = terms + jnp.dot(
                attended[h * lat_local : (h + 1) * lat_local],
                w_ref[(first + h) * HEAD_DIM : (first + h + 1) * HEAD_DIM, :],
                preferred_element_type=F32,
            )
        first += span // lat_local
    half = lat_local // 2
    terms_ref[...] = terms.reshape(2, half, w_ref.shape[1])
    own_ref[...] = terms_ref[core_ref[0]]
    other_ref[...] = terms_ref[1 - core_ref[0]].astype(BF16)


def spread_kernel(l_ref, w_ref, out_ref):
    q = jnp.dot(l_ref[...], w_ref[...], preferred_element_type=F32).astype(BF16)
    out_ref[...] = jnp.broadcast_to(q[None], out_ref.shape)


def latent_kernel(own_ref, recv_ref, w_ref, out_ref):
    normed = rms_norm(own_ref[...] + recv_ref[...].astype(F32))
    hidden = jax.nn.gelu(jnp.dot(normed.astype(BF16), w_ref[...], preferred_element_type=F32))
    rows = (normed + hidden).astype(BF16)
    out_ref[...] = jnp.broadcast_to(rows[None], out_ref.shape)


def kv_kernel(*refs):
    *row_refs, k_ref, v_ref, out_ref = refs
    at = 0
    half = k_ref.shape[1]
    for r in row_refs:
        n = r.shape[0]
        rows = r[...]
        out_ref[at : at + n, :half] = jnp.dot(rows, k_ref[...], preferred_element_type=F32).astype(BF16)
        out_ref[at : at + n, half:] = jnp.dot(rows, v_ref[...], preferred_element_type=F32).astype(BF16)
        at += n


def attend(q_ref, kv_refs, w_ref):
    columns = q_ref.shape[1]
    outs = []
    for h in range(columns // HEAD_DIM):
        kc = slice(h * HEAD_DIM, (h + 1) * HEAD_DIM)
        vc = slice(columns + h * HEAD_DIM, columns + (h + 1) * HEAD_DIM)
        q = q_ref[:, kc]
        scores = [nt_dot(q, kv[:, kc]) for kv in kv_refs]
        m = functools.reduce(jnp.maximum, [jnp.max(s, axis=1, keepdims=True) for s in scores])
        total, o = 0.0, 0.0
        for s, kv in zip(scores, kv_refs):
            p = jnp.exp2((s - m) * (SCALE * LOG2E))
            total = total + jnp.sum(p, axis=1, keepdims=True)
            o = o + jnp.dot(p.astype(BF16), kv[:, vc], preferred_element_type=F32)
        outs.append((o / total).astype(BF16))
    attended = jnp.concatenate(outs, axis=1)
    return jnp.dot(attended, w_ref[...], preferred_element_type=F32)


def decode_kernel(base_ref, q_ref, *refs):
    *kv_refs, w_ref, out_ref = refs
    out_ref[...] = attend(q_ref, kv_refs, w_ref).astype(out_ref.dtype)


def last_kernel(base_ref, q_ref, *refs):
    *kv_refs, w_ref, first_ref, recv_ref, out_ref = refs
    n = first_ref.shape[0]
    out_ref[:n] = rms_norm(first_ref[...] + recv_ref[:n].astype(F32)).astype(out_ref.dtype)
    terms = attend(q_ref, kv_refs, w_ref)
    out_ref[n:] = rms_norm(terms + recv_ref[n:].astype(F32)).astype(out_ref.dtype)


def full_spec(array):
    return pl.BlockSpec(array.shape, lambda *_: (0,) * array.ndim)


def params(limit=56 << 20):
    return pltpu.CompilerParams(vmem_limit_bytes=limit)


def cross(count, q, k, v, lat_local):
    lat, columns = q.shape
    heads = columns // HEAD_DIM
    tall = heads * lat_local + LSE_ROWS
    block = min(ROW_BLOCK, lat)
    return pl.pallas_call(
        functools.partial(cross_kernel, lat_local=lat_local),
        out_shape=jax.ShapeDtypeStruct((lat // lat_local, tall, HEAD_DIM), BF16),
        grid_spec=pltpu.PrefetchScalarGridSpec(
            num_scalar_prefetch=1,
            grid=(lat // block,),
            in_specs=[pl.BlockSpec((block, columns), lambda i, c: (i, 0)), full_spec(k), full_spec(v)],
            out_specs=pl.BlockSpec((block // lat_local, tall, HEAD_DIM), lambda i, c: (i, 0, 0)),
        ),
        compiler_params=params(32 << 20),
        cost_estimate=pl.CostEstimate(
            flops=4 * lat * k.shape[0] * columns,
            bytes_accessed=4 << 20,
            transcendentals=lat * k.shape[0] * heads,
        ),
        name="cross",
    )(count, q, k, v)


def join(parts):
    vmem = pl.BlockSpec(memory_space=pltpu.VMEM)
    return pl.pallas_call(
        join_kernel,
        out_shape=jax.ShapeDtypeStruct(parts[0].shape, BF16),
        in_specs=[vmem] * len(parts),
        out_specs=vmem,
        compiler_params=params(24 << 20),
        name="join",
    )(*parts)


def combine(core, parts, w_out, lat_local):
    width = w_out.shape[1]
    half = lat_local // 2
    vmem = pl.BlockSpec(memory_space=pltpu.VMEM)
    return pl.pallas_call(
        functools.partial(combine_kernel, lat_local=lat_local),
        out_shape=(
            jax.ShapeDtypeStruct((half, width), F32),
            jax.ShapeDtypeStruct((half, width), BF16),
        ),
        in_specs=[pl.BlockSpec(memory_space=pltpu.SMEM)] + [vmem] * (len(parts) + 1),
        out_specs=(vmem, vmem),
        scratch_shapes=[pltpu.VMEM((2, half, width), F32)],
        compiler_params=params(24 << 20),
        name="combine",
    )(core, *parts, w_out)


def spread(latents, w_query, devices):
    vmem = pl.BlockSpec(memory_space=pltpu.VMEM)
    return pl.pallas_call(
        spread_kernel,
        out_shape=jax.ShapeDtypeStruct((devices, latents.shape[0], w_query.shape[1]), BF16),
        in_specs=[vmem, vmem],
        out_specs=vmem,
        compiler_params=params(24 << 20),
        name="spread",
    )(latents, w_query)


def latent_rows(own, recv, w_mlp, devices):
    vmem = pl.BlockSpec(memory_space=pltpu.VMEM)
    return pl.pallas_call(
        latent_kernel,
        out_shape=jax.ShapeDtypeStruct((devices,) + own.shape, BF16),
        in_specs=[vmem] * 3,
        out_specs=vmem,
        compiler_params=params(24 << 20),
        name="latent",
    )(own, recv, w_mlp)


def latent_kv(rows, w_lkey, w_lvalue):
    vmem = pl.BlockSpec(memory_space=pltpu.VMEM)
    total = sum(r.shape[0] for r in rows)
    wide = w_lkey.shape[1] * 2
    return pl.pallas_call(
        kv_kernel,
        out_shape=jax.ShapeDtypeStruct((total, wide), BF16),
        in_specs=[vmem] * (len(rows) + 2),
        out_specs=vmem,
        compiler_params=params(24 << 20),
        cost_estimate=pl.CostEstimate(
            flops=2 * total * wide * w_lkey.shape[0], bytes_accessed=4 << 20, transcendentals=0
        ),
        name="latent_kv",
    )(*rows, w_lkey, w_lvalue)


def decode(base, blocks, q, kvs, w_pout, dtype, finish=()):
    columns = q.shape[1]
    width = w_pout.shape[1]
    block = ROW_BLOCK
    rows = blocks * block
    out_rows = finish[1].shape[0] if finish else rows
    out_block = out_rows if finish else block
    keys = sum(kv.shape[0] for kv in kvs)
    return pl.pallas_call(
        last_kernel if finish else decode_kernel,
        out_shape=jax.ShapeDtypeStruct((out_rows, width), dtype),
        grid_spec=pltpu.PrefetchScalarGridSpec(
            num_scalar_prefetch=1,
            grid=(blocks,),
            in_specs=[
                pl.BlockSpec((block, columns), lambda i, b: (b[0] + i, 0)),
                *[full_spec(x) for x in (*kvs, w_pout, *finish)],
            ],
            out_specs=pl.BlockSpec((out_block, width), lambda i, b: (i, 0)),
        ),
        compiler_params=params(36 << 20),
        cost_estimate=pl.CostEstimate(
            flops=4 * rows * columns * keys, bytes_accessed=8 << 20, transcendentals=4 * rows * keys
        ),
        name="decode",
    )(base, q, *kvs, w_pout, *finish)


def project(a, w):
    return jnp.dot(a, w, preferred_element_type=F32).astype(BF16)


def per_device(
    inputs,
    valid_blocks,
    latents,
    w_query,
    w_key,
    w_value,
    w_out,
    w_mlp,
    w_lkey,
    w_lvalue,
    w_pquery,
    w_pout,
):
    lat_local = latents.shape[0]
    columns = w_key.shape[1]
    width = inputs.shape[1]
    core = lax.axis_index("head").astype(jnp.int32).reshape(1)
    swap = [(0, 1), (1, 0)]

    plane, long = plane_groups()

    def within_plane(x):
        return lax.all_to_all(x, AXES, 0, 0, axis_index_groups=plane)

    def along(x, shift):
        return lax.ppermute(x, AXES, long[shift % SIDE])

    queries = within_plane(spread(latents, w_query, SIDE * SIDE)).reshape(-1, columns)
    keys = project(inputs, w_key)
    values = project(inputs, w_value)
    count = jnp.sum(valid_blocks).astype(jnp.int32).reshape(1)
    queries, keys, values = lax.optimization_barrier((queries, keys, values))
    away = [along(queries, s) for s in ORDER]
    part = cross(count, queries, keys, values, lat_local)
    partials = [part]
    for s, there in zip(ORDER, away):
        part, there = lax.optimization_barrier((part, there))
        part = cross(count, there, keys, values, lat_local)
        partials.append(along(part, -s))
    gathered = within_plane(join(partials))
    own, other = combine(core, [gathered], w_out, lat_local)
    recv = lax.ppermute(other, "head", swap)
    rows = latent_rows(own, recv, w_mlp, SIDE * SIDE)
    rows, inputs = lax.optimization_barrier((rows, inputs))
    pos_queries = project(inputs, w_pquery)
    near, pos_queries = lax.optimization_barrier((within_plane(rows), pos_queries))
    near = near.reshape(-1, width)
    far = [along(near, s) for s in ORDER]
    near_kv = latent_kv([near, lax.ppermute(near, "head", swap)], w_lkey, w_lvalue)
    near_kv, *far = lax.optimization_barrier((near_kv, *far))
    far_swapped = [lax.ppermute(x, "head", swap) for x in far]
    kvs = [near_kv, latent_kv(far, w_lkey, w_lvalue), latent_kv(far_swapped, w_lkey, w_lvalue)]
    blocks = pos_queries.shape[0] // 2 // ROW_BLOCK
    terms = decode((1 - core) * blocks, blocks, pos_queries, kvs, w_pout, BF16)
    arrived = lax.ppermute(terms, "head", swap)
    first = decode(core * blocks, blocks - 1, pos_queries, kvs, w_pout, F32)
    return decode(core * blocks + blocks - 1, 1, pos_queries, kvs, w_pout, BF16, (first, arrived))


def solution(mesh):
    placed = (
        P("pos", None),
        P("pos"),
        P("pos", None),
        P(None, "head"),
        P(None, "head"),
        P(None, "head"),
        P("head", None),
        P(),
        P(None, "head"),
        P(None, "head"),
        P(None, "head"),
        P("head", None),
    )

    return jax.shard_map(
        per_device,
        mesh=mesh,
        in_specs=placed,
        out_specs=P(("pos", "head"), None),
        check_vma=False,
    )
```

```python
import functools

import jax
import jax.numpy as jnp
from jax import lax
from jax.experimental import pallas as pl
from jax.experimental.pallas import tpu as pltpu
from jax.sharding import PartitionSpec as P


HEAD_DIM = 128
BLK = 128
SCALE = HEAD_DIM ** (-0.5)
LOG2E = 1.4426950408889634
MASKED = -1e30
EPS = 1e-05
F32 = jnp.float32
BF16 = jnp.bfloat16
ROW_BLOCK = 256
LSE_ROWS = 8


AXES = ("pos", "head")
SIDE = 4
ORDER = (1, 2, 3)


def plane_groups():
    def device(z, y, x, core):
        return ((z * SIDE + y) * SIDE + x) * 2 + core

    r = range(SIDE)
    plane = [[device(z, y, x, 0) for y in r for x in r] for z in r]
    plane += [[device(z, y, x, 1) for z in r for x in r] for y in r]
    long = {}
    for s in range(1, SIDE):
        long[s] = [
            pair
            for z in r
            for y in r
            for x in r
            for pair in (
                (device(z, y, x, 0), device((z + s) % SIDE, y, x, 0)),
                (device(z, y, x, 1), device(z, (y + s) % SIDE, x, 1)),
            )
        ]
    return plane, long


def rms_norm(values):
    return values * lax.rsqrt(jnp.mean(values * values, axis=-1, keepdims=True) + EPS)


def nt_dot(a, b):
    return lax.dot_general(a, b, (((1,), (1,)), ((), ())), preferred_element_type=F32)


def pieces(row):
    hi = row.astype(BF16).astype(F32)
    mid = (row - hi).astype(BF16).astype(F32)
    low = (row - hi - mid).astype(BF16).astype(F32)
    place = lax.broadcasted_iota(jnp.int32, row.shape, 0)
    packed = jnp.where(place == 0, hi, jnp.where(place == 1, mid, jnp.where(place == 2, low, 0.0)))
    return packed.astype(BF16)


def cross_kernel(valid_ref, q_ref, k_ref, v_ref, *refs, lat_local, first, heads):
    before_ref, out_ref = refs if len(refs) == 2 else (None, refs[0])
    rows = q_ref.shape[0]
    owners = rows // lat_local
    done = first * lat_local
    span = done + heads * lat_local
    keys = k_ref.shape[0]
    valid = sum(valid_ref[i] for i in range(keys // BLK)) * BLK
    live = lax.broadcasted_iota(jnp.int32, (1, keys), 1) < valid
    bias = jnp.where(live, 0.0, MASKED)
    if before_ref is not None:
        out_ref[:, :done, :] = before_ref[:, :done, :]
    zeros = jnp.zeros((rows, 1), F32)
    columns = [zeros] * first
    for h in range(first, first + heads):
        cols = slice(h * HEAD_DIM, (h + 1) * HEAD_DIM)
        s = nt_dot(q_ref[:, cols], k_ref[:, cols]) + bias
        m = jnp.max(s, axis=1, keepdims=True)
        p = jnp.exp2((s - m) * (SCALE * LOG2E))
        total = jnp.sum(p, axis=1, keepdims=True)
        o = jnp.dot(p.astype(BF16), v_ref[:, cols], preferred_element_type=F32)
        o = (o / total).astype(BF16)
        out_ref[:, h * lat_local : (h + 1) * lat_local, :] = o.reshape(owners, lat_local, HEAD_DIM)
        columns.append(m * SCALE + jnp.log(total))
    columns += [zeros] * (HEAD_DIM // lat_local - len(columns))
    for d in range(owners):
        part = jnp.concatenate([c[d * lat_local : (d + 1) * lat_local] for c in columns], axis=0)
        row = jnp.transpose(jnp.broadcast_to(part, (HEAD_DIM, HEAD_DIM)))[:LSE_ROWS]
        packed = pieces(row)
        if before_ref is not None:
            packed = packed + before_ref[d, done : done + LSE_ROWS, :]
        out_ref[d, span : span + LSE_ROWS, :] = packed


def load_kernel(*refs):
    n = len(refs) // 2
    *pairs, sems = refs
    copies = [pltpu.make_async_copy(pairs[i], pairs[n + i], sems.at[i]) for i in range(n)]
    for copy in copies:
        copy.start()
    for copy in copies:
        copy.wait()


def join_kernel(*refs):
    *parts, out_ref = refs
    owners, tall, _ = out_ref.shape
    span = tall - LSE_ROWS
    lses = [jnp.sum(r[:, span : span + LSE_ROWS, :].astype(F32), axis=1) for r in parts]
    top = functools.reduce(jnp.maximum, lses)
    ws = [jnp.exp(x - top) for x in lses]
    total = functools.reduce(jnp.add, ws)
    lse = top + jnp.log(total)
    wts = [jnp.transpose(w / total) for w in ws]
    for d in range(owners):
        acc = jnp.zeros((span, HEAD_DIM), F32)
        for wt, r in zip(wts, parts):
            acc = acc + wt[:, d : d + 1] * r[d, :span, :].astype(F32)
        out_ref[d, :span, :] = acc.astype(BF16)
        row = jnp.broadcast_to(lse[d : d + 1, :], (LSE_ROWS, HEAD_DIM))
        out_ref[d, span : span + LSE_ROWS, :] = pieces(row)


def combine_kernel(core_ref, r_ref, w_ref, mlp_ref, own_ref, other_ref, mlp_out, terms_ref, w_vmem, sems, *, lat_local):
    copies = [
        pltpu.make_async_copy(w_ref, w_vmem, sems.at[0]),
        pltpu.make_async_copy(mlp_ref, mlp_out, sems.at[1]),
    ]
    for copy in copies:
        copy.start()
    devices, tall, _ = r_ref.shape
    span = tall - LSE_ROWS
    lse = jnp.sum(r_ref[:, span : span + LSE_ROWS, :].astype(F32), axis=1)
    w = jnp.exp(lse - jnp.max(lse, axis=0, keepdims=True))
    w = w / jnp.sum(w, axis=0, keepdims=True)
    wt = jnp.transpose(w)
    acc = jnp.zeros((span, HEAD_DIM), F32)
    for d in range(devices):
        acc = acc + wt[:span, d : d + 1] * r_ref[d, :span, :].astype(F32)
    attended = acc.astype(BF16)
    copies[0].wait()
    terms = jnp.zeros((lat_local, w_vmem.shape[1]), F32)
    for h in range(span // lat_local):
        terms = terms + jnp.dot(
            attended[h * lat_local : (h + 1) * lat_local],
            w_vmem[h * HEAD_DIM : (h + 1) * HEAD_DIM, :],
            preferred_element_type=F32,
        )
    half = lat_local // 2
    terms_ref[...] = terms.reshape(2, half, w_vmem.shape[1])
    own_ref[...] = terms_ref[core_ref[0]]
    other_ref[...] = terms_ref[1 - core_ref[0]].astype(BF16)
    copies[1].wait()


def spread_kernel(l_ref, w_ref, out_ref, l_vmem, w_vmem, sems):
    copies = [
        pltpu.make_async_copy(w_ref, w_vmem, sems.at[0]),
        pltpu.make_async_copy(l_ref, l_vmem, sems.at[1]),
    ]
    for copy in copies:
        copy.start()
    for copy in copies:
        copy.wait()
    q = jnp.dot(l_vmem[...], w_vmem[...], preferred_element_type=F32).astype(BF16)
    out_ref[...] = jnp.broadcast_to(q[None], out_ref.shape)


def latent_kernel(own_ref, recv_ref, w_ref, out_ref):
    normed = rms_norm(own_ref[...] + recv_ref[...].astype(F32))
    hidden = jax.nn.gelu(jnp.dot(normed.astype(BF16), w_ref[...], preferred_element_type=F32))
    rows = (normed + hidden).astype(BF16)
    out_ref[...] = jnp.broadcast_to(rows[None], out_ref.shape)


def write_kv(row_refs, w_ref, out_ref, first):
    at = 0
    wide = w_ref.shape[1]
    for r in row_refs:
        n = r.shape[0]
        out_ref[at : at + n, first : first + wide] = jnp.dot(
            r[...], w_ref[...], preferred_element_type=F32
        ).astype(BF16)
        at += n


def kv_kernel(*refs):
    *row_refs, k_ref, v_ref, out_ref = refs
    write_kv(row_refs, k_ref, out_ref, 0)
    write_kv(row_refs, v_ref, out_ref, k_ref.shape[1])


def near_kv_kernel(near_ref, swapped_ref, k_ref, v_ref, p_ref, out_ref, k_out, v_out, p_out, sems):
    pairs = ((k_ref, k_out), (v_ref, v_out), (p_ref, p_out))
    copies = [pltpu.make_async_copy(a, b, sems.at[i]) for i, (a, b) in enumerate(pairs)]
    for copy in copies:
        copy.start()
    rows = (near_ref, swapped_ref)
    copies[0].wait()
    write_kv(rows, k_out, out_ref, 0)
    copies[1].wait()
    write_kv(rows, v_out, out_ref, k_out.shape[1])
    copies[2].wait()


def head_columns(columns, h):
    return (
        slice(h * HEAD_DIM, (h + 1) * HEAD_DIM),
        slice(columns + h * HEAD_DIM, columns + (h + 1) * HEAD_DIM),
    )


def near_kernel(q_ref, kv_ref, sums_ref, stats_ref):
    columns = q_ref.shape[1]
    heads = columns // HEAD_DIM
    for h in range(heads):
        kc, vc = head_columns(columns, h)
        s = nt_dot(q_ref[:, kc], kv_ref[:, kc])
        m = jnp.max(s, axis=1, keepdims=True)
        p = jnp.exp2((s - m) * (SCALE * LOG2E))
        sums_ref[:, kc] = jnp.dot(p.astype(BF16), kv_ref[:, vc], preferred_element_type=F32)
        stats_ref[:, h : h + 1] = m
        stats_ref[:, heads + h : heads + h + 1] = jnp.sum(p, axis=1, keepdims=True)


def attend(q_ref, sums_ref, stats_ref, kv_refs, w_ref):
    columns = q_ref.shape[1]
    heads = columns // HEAD_DIM
    outs = []
    for h in range(heads):
        kc, vc = head_columns(columns, h)
        q = q_ref[:, kc]
        scores = [nt_dot(q, kv[:, kc]) for kv in kv_refs]
        before = stats_ref[:, h : h + 1]
        m = functools.reduce(jnp.maximum, [before, *[jnp.max(s, axis=1, keepdims=True) for s in scores]])
        keep = jnp.exp2((before - m) * (SCALE * LOG2E))
        total = stats_ref[:, heads + h : heads + h + 1] * keep
        o = sums_ref[:, kc] * keep
        for s, kv in zip(scores, kv_refs):
            p = jnp.exp2((s - m) * (SCALE * LOG2E))
            total = total + jnp.sum(p, axis=1, keepdims=True)
            o = o + jnp.dot(p.astype(BF16), kv[:, vc], preferred_element_type=F32)
        outs.append((o / total).astype(BF16))
    attended = jnp.concatenate(outs, axis=1)
    return jnp.dot(attended, w_ref[...], preferred_element_type=F32)


def decode_kernel(base_ref, q_ref, sums_ref, stats_ref, *refs):
    *kv_refs, w_ref, out_ref = refs
    out_ref[...] = attend(q_ref, sums_ref, stats_ref, kv_refs, w_ref).astype(out_ref.dtype)


def last_kernel(base_ref, q_ref, sums_ref, stats_ref, *refs):
    *kv_refs, w_ref, first_ref, recv_ref, out_ref = refs
    n = first_ref.shape[0]
    out_ref[:n] = rms_norm(first_ref[...] + recv_ref[:n].astype(F32)).astype(out_ref.dtype)
    terms = attend(q_ref, sums_ref, stats_ref, kv_refs, w_ref)
    out_ref[n:] = rms_norm(terms + recv_ref[n:].astype(F32)).astype(out_ref.dtype)


def full_spec(array):
    return pl.BlockSpec(array.shape, lambda *_: (0,) * array.ndim)


def params(limit=56 << 20):
    return pltpu.CompilerParams(vmem_limit_bytes=limit)


def cross(valid, q, k, v, lat_local, first, heads, before=None):
    lat, columns = q.shape
    tall = (first + heads) * lat_local + LSE_ROWS
    block = min(ROW_BLOCK, lat)
    extra = () if before is None else (before,)
    return pl.pallas_call(
        functools.partial(cross_kernel, lat_local=lat_local, first=first, heads=heads),
        out_shape=jax.ShapeDtypeStruct((lat // lat_local, tall, HEAD_DIM), BF16),
        grid_spec=pltpu.PrefetchScalarGridSpec(
            num_scalar_prefetch=1,
            grid=(lat // block,),
            in_specs=[
                pl.BlockSpec((block, columns), lambda i, c: (i, 0)),
                full_spec(k),
                full_spec(v),
                *[pl.BlockSpec((block // lat_local,) + x.shape[1:], lambda i, c: (i, 0, 0)) for x in extra],
            ],
            out_specs=pl.BlockSpec((block // lat_local, tall, HEAD_DIM), lambda i, c: (i, 0, 0)),
        ),
        compiler_params=params(32 << 20),
        cost_estimate=pl.CostEstimate(
            flops=4 * lat * k.shape[0] * heads * HEAD_DIM,
            bytes_accessed=4 << 20,
            transcendentals=lat * k.shape[0] * heads,
        ),
        name="cross",
    )(valid, q, k, v, *extra)


def in_hbm(*arrays):
    return [pltpu.with_memory_space_constraint(x, pltpu.HBM) for x in arrays]


def load(arrays):
    return pl.pallas_call(
        load_kernel,
        out_shape=[jax.ShapeDtypeStruct(x.shape, x.dtype) for x in arrays],
        in_specs=[pl.BlockSpec(memory_space=pltpu.HBM)] * len(arrays),
        out_specs=[pl.BlockSpec(memory_space=pltpu.VMEM)] * len(arrays),
        scratch_shapes=[pltpu.SemaphoreType.DMA((len(arrays),))],
        compiler_params=params(8 << 20),
        name="load",
    )(*in_hbm(*arrays))


def join(parts):
    vmem = pl.BlockSpec(memory_space=pltpu.VMEM)
    return pl.pallas_call(
        join_kernel,
        out_shape=jax.ShapeDtypeStruct(parts[0].shape, BF16),
        in_specs=[vmem] * len(parts),
        out_specs=vmem,
        compiler_params=params(24 << 20),
        name="join",
    )(*parts)


def combine(core, gathered, w_out, w_mlp, lat_local):
    width = w_out.shape[1]
    half = lat_local // 2
    vmem = pl.BlockSpec(memory_space=pltpu.VMEM)
    hbm = pl.BlockSpec(memory_space=pltpu.HBM)
    return pl.pallas_call(
        functools.partial(combine_kernel, lat_local=lat_local),
        out_shape=(
            jax.ShapeDtypeStruct((half, width), F32),
            jax.ShapeDtypeStruct((half, width), BF16),
            jax.ShapeDtypeStruct(w_mlp.shape, BF16),
        ),
        in_specs=[pl.BlockSpec(memory_space=pltpu.SMEM), vmem, hbm, hbm],
        out_specs=(vmem, vmem, vmem),
        scratch_shapes=[
            pltpu.VMEM((2, half, width), F32),
            pltpu.VMEM(w_out.shape, BF16),
            pltpu.SemaphoreType.DMA((2,)),
        ],
        compiler_params=params(24 << 20),
        name="combine",
    )(core, gathered, *in_hbm(w_out, w_mlp))


def spread(latents, w_query, devices):
    hbm = pl.BlockSpec(memory_space=pltpu.HBM)
    return pl.pallas_call(
        spread_kernel,
        out_shape=jax.ShapeDtypeStruct((devices, latents.shape[0], w_query.shape[1]), BF16),
        in_specs=[hbm, hbm],
        out_specs=pl.BlockSpec(memory_space=pltpu.VMEM),
        scratch_shapes=[
            pltpu.VMEM(latents.shape, BF16),
            pltpu.VMEM(w_query.shape, BF16),
            pltpu.SemaphoreType.DMA((2,)),
        ],
        compiler_params=params(60 << 20),
        name="spread",
    )(*in_hbm(latents, w_query))


def latent_rows(own, recv, w_mlp, devices):
    vmem = pl.BlockSpec(memory_space=pltpu.VMEM)
    return pl.pallas_call(
        latent_kernel,
        out_shape=jax.ShapeDtypeStruct((devices,) + own.shape, BF16),
        in_specs=[vmem] * 3,
        out_specs=vmem,
        compiler_params=params(24 << 20),
        name="latent",
    )(own, recv, w_mlp)


def latent_kv(rows, w_lkey, w_lvalue):
    vmem = pl.BlockSpec(memory_space=pltpu.VMEM)
    total = sum(r.shape[0] for r in rows)
    wide = w_lkey.shape[1] * 2
    return pl.pallas_call(
        kv_kernel,
        out_shape=jax.ShapeDtypeStruct((total, wide), BF16),
        in_specs=[vmem] * (len(rows) + 2),
        out_specs=vmem,
        compiler_params=params(24 << 20),
        cost_estimate=pl.CostEstimate(
            flops=2 * total * wide * w_lkey.shape[0], bytes_accessed=4 << 20, transcendentals=0
        ),
        name="latent_kv",
    )(*rows, w_lkey, w_lvalue)


def near_kv(near, swapped, w_lkey, w_lvalue, w_pout):
    vmem = pl.BlockSpec(memory_space=pltpu.VMEM)
    hbm = pl.BlockSpec(memory_space=pltpu.HBM)
    rows = near.shape[0] + swapped.shape[0]
    return pl.pallas_call(
        near_kv_kernel,
        out_shape=[
            jax.ShapeDtypeStruct((rows, 2 * w_lkey.shape[1]), BF16),
            *[jax.ShapeDtypeStruct(w.shape, BF16) for w in (w_lkey, w_lvalue, w_pout)],
        ],
        in_specs=[vmem, vmem, hbm, hbm, hbm],
        out_specs=[vmem] * 4,
        scratch_shapes=[pltpu.SemaphoreType.DMA((3,))],
        compiler_params=params(24 << 20),
        cost_estimate=pl.CostEstimate(
            flops=4 * rows * w_lkey.size // 2, bytes_accessed=4 << 20, transcendentals=0
        ),
        name="near_kv",
    )(near, swapped, *in_hbm(w_lkey, w_lvalue, w_pout))


def near_decode(q, kv):
    rows, columns = q.shape
    block = ROW_BLOCK
    return pl.pallas_call(
        near_kernel,
        out_shape=(
            jax.ShapeDtypeStruct((rows, columns), F32),
            jax.ShapeDtypeStruct((rows, HEAD_DIM), F32),
        ),
        grid=(rows // block,),
        in_specs=[pl.BlockSpec((block, columns), lambda i: (i, 0)), full_spec(kv)],
        out_specs=(
            pl.BlockSpec((block, columns), lambda i: (i, 0)),
            pl.BlockSpec((block, HEAD_DIM), lambda i: (i, 0)),
        ),
        compiler_params=params(24 << 20),
        cost_estimate=pl.CostEstimate(
            flops=4 * rows * columns * kv.shape[0], bytes_accessed=4 << 20, transcendentals=4 * rows * kv.shape[0]
        ),
        name="near_decode",
    )(q, kv)


def decode(base, blocks, q, carried, kvs, w_pout, dtype, finish=()):
    columns = q.shape[1]
    width = w_pout.shape[1]
    block = ROW_BLOCK
    rows = blocks * block
    out_rows = finish[1].shape[0] if finish else rows
    out_block = out_rows if finish else block
    keys = sum(kv.shape[0] for kv in kvs)
    return pl.pallas_call(
        last_kernel if finish else decode_kernel,
        out_shape=jax.ShapeDtypeStruct((out_rows, width), dtype),
        grid_spec=pltpu.PrefetchScalarGridSpec(
            num_scalar_prefetch=1,
            grid=(blocks,),
            in_specs=[
                *[pl.BlockSpec((block, x.shape[1]), lambda i, b: (b[0] + i, 0)) for x in (q, *carried)],
                *[full_spec(x) for x in (*kvs, w_pout, *finish)],
            ],
            out_specs=pl.BlockSpec((out_block, width), lambda i, b: (i, 0)),
        ),
        compiler_params=params(36 << 20),
        cost_estimate=pl.CostEstimate(
            flops=4 * rows * columns * keys, bytes_accessed=8 << 20, transcendentals=4 * rows * keys
        ),
        name="decode",
    )(base, q, *carried, *kvs, w_pout, *finish)


def project(a, w):
    return jnp.dot(a, w, preferred_element_type=F32).astype(BF16)


def per_device(
    inputs,
    valid_blocks,
    latents,
    w_query,
    w_key,
    w_value,
    w_out,
    w_mlp,
    w_lkey,
    w_lvalue,
    w_pquery,
    w_pout,
):
    lat_local = latents.shape[0]
    columns = w_key.shape[1]
    width = inputs.shape[1]
    core = lax.axis_index("head").astype(jnp.int32).reshape(1)
    swap = [(0, 1), (1, 0)]

    plane, long = plane_groups()

    def within_plane(x):
        return lax.all_to_all(x, AXES, 0, 0, axis_index_groups=plane)

    def along(x, shift):
        return lax.ppermute(x, AXES, long[shift % SIDE])

    queries = within_plane(spread(latents, w_query, SIDE * SIDE)).reshape(-1, columns)
    keys = project(inputs, w_key)
    values = project(inputs, w_value)
    queries, keys, values = lax.optimization_barrier((queries, keys, values))
    away = [along(queries, s) for s in ORDER]
    keys, values = load((keys, values))
    heads = columns // HEAD_DIM
    half = cross(valid_blocks, queries, keys, values, lat_local, 0, heads // 2)
    part, partials = half, []
    for s, there in zip(ORDER, away):
        part, there = lax.optimization_barrier((part, there))
        part = cross(valid_blocks, there, keys, values, lat_local, 0, heads)
        partials.append(along(part, -s))
    part, half = lax.optimization_barrier((part, half))
    partials.append(cross(valid_blocks, queries, keys, values, lat_local, heads // 2, heads // 2, half))
    gathered = within_plane(join(partials))
    own, other, w_mlp = combine(core, gathered, w_out, w_mlp, lat_local)
    recv = lax.ppermute(other, "head", swap)
    rows = latent_rows(own, recv, w_mlp, SIDE * SIDE)
    rows, inputs = lax.optimization_barrier((rows, inputs))
    pos_queries = project(inputs, w_pquery)
    near, pos_queries = lax.optimization_barrier((within_plane(rows), pos_queries))
    near = near.reshape(-1, width)
    far = [along(near, s) for s in ORDER]
    kv, w_lkey, w_lvalue, w_pout = near_kv(near, lax.ppermute(near, "head", swap), w_lkey, w_lvalue, w_pout)
    carried = near_decode(pos_queries, kv)
    carried, far = lax.optimization_barrier((carried, far))
    far_swapped = [lax.ppermute(x, "head", swap) for x in far]
    kvs = [latent_kv(far, w_lkey, w_lvalue), latent_kv(far_swapped, w_lkey, w_lvalue)]
    blocks = pos_queries.shape[0] // 2 // ROW_BLOCK
    terms = decode((1 - core) * blocks, blocks, pos_queries, carried, kvs, w_pout, BF16)
    arrived = lax.ppermute(terms, "head", swap)
    first = decode(core * blocks, blocks - 1, pos_queries, carried, kvs, w_pout, F32)
    return decode(core * blocks + blocks - 1, 1, pos_queries, carried, kvs, w_pout, BF16, (first, arrived))


def solution(mesh):
    placed = (
        P("pos", None),
        P("pos"),
        P("pos", None),
        P(None, "head"),
        P(None, "head"),
        P(None, "head"),
        P("head", None),
        P(),
        P(None, "head"),
        P(None, "head"),
        P(None, "head"),
        P("head", None),
    )

    return jax.shard_map(
        per_device,
        mesh=mesh,
        in_specs=placed,
        out_specs=P(("pos", "head"), None),
        check_vma=False,
    )
```

```python
import functools

import jax
import jax.numpy as jnp
from jax import lax
from jax.experimental import pallas as pl
from jax.experimental.pallas import tpu as pltpu
from jax.sharding import PartitionSpec as P


HEAD_DIM = 128
BLK = 128
SCALE = HEAD_DIM ** (-0.5)
LOG2E = 1.4426950408889634
MASKED = -1e30
EPS = 1e-05
F32 = jnp.float32
BF16 = jnp.bfloat16
ROW_BLOCK = 256
LSE_ROWS = 16


AXES = ("pos", "head")
SIDE = 4
ORDER = (1, 2, 3)


def plane_groups():
    def device(z, y, x, core):
        return ((z * SIDE + y) * SIDE + x) * 2 + core

    r = range(SIDE)
    plane = [[device(z, y, x, 0) for y in r for x in r] for z in r]
    plane += [[device(z, y, x, 1) for z in r for x in r] for y in r]
    long = {}
    for s in range(1, SIDE):
        long[s] = [
            pair
            for z in r
            for y in r
            for x in r
            for pair in (
                (device(z, y, x, 0), device((z + s) % SIDE, y, x, 0)),
                (device(z, y, x, 1), device(z, (y + s) % SIDE, x, 1)),
            )
        ]
    return plane, long


def lane_offset(lat_local):
    x = lax.axis_index("pos") % SIDE
    return (x % (HEAD_DIM // lat_local) * lat_local).astype(jnp.int32).reshape(1)


def rms_norm(values):
    return values * lax.rsqrt(jnp.mean(values * values, axis=-1, keepdims=True) + EPS)


def nt_dot(a, b):
    return lax.dot_general(a, b, (((1,), (1,)), ((), ())), preferred_element_type=F32)


def bf16_pieces(x):
    hi = x.astype(BF16).astype(F32)
    mid = (x - hi).astype(BF16).astype(F32)
    low = (x - hi - mid).astype(BF16).astype(F32)
    return hi, mid, low


def pack_rows(lse, heads):
    rows = jnp.concatenate([p[:heads] for p in bf16_pieces(lse)], axis=0)
    pad = jnp.zeros((LSE_ROWS - rows.shape[0], rows.shape[1]), F32)
    return jnp.concatenate([rows, pad], axis=0).astype(BF16)


def unpack_rows(packed, heads):
    x = packed.astype(F32)
    return x[:heads] + x[heads : 2 * heads] + x[2 * heads : 3 * heads]


def pipelined(count, score, use):
    score(0)
    for i in range(count):
        if i + 1 < count:
            score(i + 1)
        use(i)


def cross_kernel(valid_ref, q_ref, k_ref, v_ref, *refs, lat_local, first, heads):
    *before, out_ref, s_ref = refs
    rows = q_ref.shape[0]
    owners = rows // lat_local
    all_heads = q_ref.shape[1] // HEAD_DIM
    done = first * lat_local
    span = done + heads * lat_local
    keys = k_ref.shape[0]
    valid = sum(valid_ref[i] for i in range(keys // BLK)) * BLK
    live = lax.broadcasted_iota(jnp.int32, (1, keys), 1) < valid
    bias = jnp.where(live, 0.0, MASKED)
    lane = lax.broadcasted_iota(jnp.int32, (rows, HEAD_DIM), 1)
    if before:
        out_ref[:, :done, :] = before[0][:, :done, :]
    tops = jnp.zeros((rows, HEAD_DIM), F32)
    totals = jnp.ones((rows, HEAD_DIM), F32)

    def columns(i):
        return slice((first + i) * HEAD_DIM, (first + i + 1) * HEAD_DIM)

    def score(i):
        s_ref[i % 2] = nt_dot(q_ref[:, columns(i)], k_ref[:, columns(i)]) + bias

    def use(i):
        nonlocal tops, totals
        s = s_ref[i % 2]
        m = jnp.max(s, axis=1, keepdims=True)
        p = jnp.exp2((s - m) * (SCALE * LOG2E))
        total = jnp.sum(p, axis=1, keepdims=True)
        o = jnp.dot(p.astype(BF16), v_ref[:, columns(i)], preferred_element_type=F32)
        o = (o / total).astype(BF16)
        top = (first + i) * lat_local
        out_ref[:, top : top + lat_local, :] = o.reshape(owners, lat_local, HEAD_DIM)
        mine = lane % all_heads == first + i
        tops = jnp.where(mine, m, tops)
        totals = jnp.where(mine, total, totals)

    pipelined(heads, score, use)
    hi, mid, low = bf16_pieces(tops * SCALE + jnp.log(totals))
    place = lane // all_heads
    packed = jnp.where(place == 0, hi, jnp.where(place == 1, mid, jnp.where(place == 2, low, 0.0)))
    eye = lax.broadcasted_iota(jnp.int32, (LSE_ROWS, HEAD_DIM), 0)
    eye = (eye == lax.broadcasted_iota(jnp.int32, (LSE_ROWS, HEAD_DIM), 1)).astype(BF16)
    turned = nt_dot(eye, packed.astype(BF16)).astype(BF16)
    for d in range(owners):
        at = d * lat_local // HEAD_DIM * HEAD_DIM
        rows_d = turned[:, at : at + HEAD_DIM]
        if before:
            rows_d = rows_d + before[0][d, done : done + LSE_ROWS, :]
        out_ref[d, span : span + LSE_ROWS, :] = rows_d


def load_kernel(*refs):
    n = len(refs) // 2
    *pairs, sems = refs
    copies = [pltpu.make_async_copy(pairs[i], pairs[n + i], sems.at[i]) for i in range(n)]
    for copy in copies:
        copy.start()
    for copy in copies:
        copy.wait()


def join_kernel(*refs, lat_local):
    *parts, out_ref = refs
    owners, tall, _ = out_ref.shape
    span = tall - LSE_ROWS
    heads = span // lat_local
    group = HEAD_DIM // lat_local
    for g in range(0, owners, group):
        lses = [unpack_rows(r[g, span : span + LSE_ROWS, :], heads) for r in parts]
        top = functools.reduce(jnp.maximum, lses)
        ws = [jnp.exp(x - top) for x in lses]
        total = functools.reduce(jnp.add, ws)
        packed = pack_rows(top + jnp.log(total), heads)
        stacked = jnp.concatenate([w / total for w in ws], axis=0)
        wt = jnp.transpose(stacked)
        for d in range(group):
            out_ref[g + d, span : span + LSE_ROWS, :] = packed
            for h in range(heads):
                rows = slice(h * lat_local, (h + 1) * lat_local)
                acc = jnp.zeros((lat_local, HEAD_DIM), F32)
                for i, r in enumerate(parts):
                    w = wt[d * lat_local : (d + 1) * lat_local, i * heads + h : i * heads + h + 1]
                    acc = acc + w * r[g + d, rows, :].astype(F32)
                out_ref[g + d, rows, :] = acc.astype(BF16)


def combine_kernel(core_ref, r_ref, w_ref, mlp_ref, own_ref, other_ref, mlp_out, terms_ref, spot_ref, w_vmem, sems, *, lat_local):
    copies = [
        pltpu.make_async_copy(w_ref, w_vmem, sems.at[0]),
        pltpu.make_async_copy(mlp_ref, mlp_out, sems.at[1]),
    ]
    for copy in copies:
        copy.start()
    devices, tall, _ = r_ref.shape
    span = tall - LSE_ROWS
    heads = span // lat_local
    lses = [unpack_rows(r_ref[d, span : span + LSE_ROWS, :], heads) for d in range(devices)]
    top = functools.reduce(jnp.maximum, lses)
    ws = [jnp.exp(x - top) for x in lses]
    total = functools.reduce(jnp.add, ws)
    stacked = jnp.concatenate([w / total for w in ws], axis=0)
    spot_ref[...] = jnp.transpose(stacked)
    wt = spot_ref[pl.ds(pl.multiple_of(core_ref[1], lat_local), lat_local), :]
    parts = []
    for h in range(heads):
        acc = jnp.zeros((lat_local, HEAD_DIM), F32)
        for d in range(devices):
            w = wt[:, d * heads + h : d * heads + h + 1]
            acc = acc + w * r_ref[d, h * lat_local : (h + 1) * lat_local, :].astype(F32)
        parts.append(acc.astype(BF16))
    copies[0].wait()
    terms = jnp.zeros((lat_local, w_vmem.shape[1]), F32)
    for h in range(span // lat_local):
        terms = terms + jnp.dot(
            parts[h],
            w_vmem[h * HEAD_DIM : (h + 1) * HEAD_DIM, :],
            preferred_element_type=F32,
        )
    half = lat_local // 2
    terms_ref[...] = terms.reshape(2, half, w_vmem.shape[1])
    own_ref[...] = terms_ref[core_ref[0]]
    other_ref[...] = terms_ref[1 - core_ref[0]].astype(BF16)
    copies[1].wait()


def spread_kernel(l_ref, w_ref, out_ref, l_vmem, w_vmem, sems):
    copies = [
        pltpu.make_async_copy(w_ref, w_vmem, sems.at[0]),
        pltpu.make_async_copy(l_ref, l_vmem, sems.at[1]),
    ]
    for copy in copies:
        copy.start()
    for copy in copies:
        copy.wait()
    q = jnp.dot(l_vmem[...], w_vmem[...], preferred_element_type=F32).astype(BF16)
    out_ref[...] = jnp.broadcast_to(q[None], out_ref.shape)


def latent_kernel(own_ref, recv_ref, w_ref, out_ref):
    normed = rms_norm(own_ref[...] + recv_ref[...].astype(F32))
    hidden = jax.nn.gelu(jnp.dot(normed.astype(BF16), w_ref[...], preferred_element_type=F32))
    rows = (normed + hidden).astype(BF16)
    out_ref[...] = jnp.broadcast_to(rows[None], out_ref.shape)


def write_kv(row_refs, w_ref, out_ref, first):
    at = 0
    wide = w_ref.shape[1]
    for r in row_refs:
        n = r.shape[0]
        out_ref[at : at + n, first : first + wide] = jnp.dot(
            r[...], w_ref[...], preferred_element_type=F32
        ).astype(BF16)
        at += n


def kv_kernel(*refs):
    *row_refs, k_ref, v_ref, out_ref = refs
    write_kv(row_refs, k_ref, out_ref, 0)
    write_kv(row_refs, v_ref, out_ref, k_ref.shape[1])


def near_kv_kernel(near_ref, swapped_ref, k_ref, v_ref, p_ref, out_ref, k_out, v_out, p_out, sems):
    pairs = ((k_ref, k_out), (v_ref, v_out), (p_ref, p_out))
    copies = [pltpu.make_async_copy(a, b, sems.at[i]) for i, (a, b) in enumerate(pairs)]
    for copy in copies:
        copy.start()
    rows = (near_ref, swapped_ref)
    copies[0].wait()
    write_kv(rows, k_out, out_ref, 0)
    copies[1].wait()
    write_kv(rows, v_out, out_ref, k_out.shape[1])
    copies[2].wait()


def head_columns(columns, h):
    return (
        slice(h * HEAD_DIM, (h + 1) * HEAD_DIM),
        slice(columns + h * HEAD_DIM, columns + (h + 1) * HEAD_DIM),
    )


def near_kernel(q_ref, kv_ref, sums_ref, tops_ref, totals_ref, s_ref):
    columns = q_ref.shape[1]
    shape = (q_ref.shape[0], HEAD_DIM)

    def score(h):
        kc, _ = head_columns(columns, h)
        s_ref[h % 2] = nt_dot(q_ref[:, kc], kv_ref[:, kc])

    def use(h):
        kc, vc = head_columns(columns, h)
        s = s_ref[h % 2]
        m = jnp.max(s, axis=1, keepdims=True)
        p = jnp.exp2((s - m) * (SCALE * LOG2E))
        sums_ref[:, kc] = jnp.dot(p.astype(BF16), kv_ref[:, vc], preferred_element_type=F32)
        tops_ref[:, kc] = jnp.broadcast_to(m, shape)
        totals_ref[:, kc] = jnp.broadcast_to(jnp.sum(p, axis=1, keepdims=True), shape)

    pipelined(columns // HEAD_DIM, score, use)


def attend(q_ref, carried_refs, kv_refs, w_ref, s_ref, o_ref):
    sums_ref, tops_ref, totals_ref = carried_refs
    columns = q_ref.shape[1]
    spots = []
    at = 0
    for kv in kv_refs:
        spots.append(slice(at, at + kv.shape[0]))
        at += kv.shape[0]

    def score(h):
        kc, _ = head_columns(columns, h)
        for spot, kv in zip(spots, kv_refs):
            s_ref[h % 2, :, spot] = nt_dot(q_ref[:, kc], kv[:, kc])

    def use(h):
        kc, vc = head_columns(columns, h)
        s = s_ref[h % 2]
        before = tops_ref[:, kc]
        m = jnp.maximum(before, jnp.max(s, axis=1, keepdims=True))
        keep = jnp.exp2((before - m) * (SCALE * LOG2E))
        p = jnp.exp2((s - m[:, :1]) * (SCALE * LOG2E))
        total = totals_ref[:, kc] * keep + jnp.sum(p, axis=1, keepdims=True)
        o = sums_ref[:, kc] * keep
        pb = p.astype(BF16)
        for spot, kv in zip(spots, kv_refs):
            o = o + jnp.dot(pb[:, spot], kv[:, vc], preferred_element_type=F32)
        o_ref[:, kc] = (o / total).astype(BF16)

    pipelined(columns // HEAD_DIM, score, use)
    return jnp.dot(o_ref[...], w_ref[...], preferred_element_type=F32)


def decode_kernel(base_ref, q_ref, *refs):
    *carried, kv_a, kv_b, w_ref, out_ref, s_ref, o_ref = refs
    out_ref[...] = attend(q_ref, carried, (kv_a, kv_b), w_ref, s_ref, o_ref).astype(out_ref.dtype)


def last_kernel(base_ref, q_ref, *refs):
    *carried, kv_a, kv_b, w_ref, first_ref, recv_ref, out_ref, s_ref, o_ref = refs
    n = first_ref.shape[0]
    out_ref[:n] = rms_norm(first_ref[...] + recv_ref[:n].astype(F32)).astype(out_ref.dtype)
    terms = attend(q_ref, carried, (kv_a, kv_b), w_ref, s_ref, o_ref)
    out_ref[n:] = rms_norm(terms + recv_ref[n:].astype(F32)).astype(out_ref.dtype)


def full_spec(array):
    return pl.BlockSpec(array.shape, lambda *_: (0,) * array.ndim)


def params(limit=56 << 20):
    return pltpu.CompilerParams(vmem_limit_bytes=limit)


def cross(valid, q, k, v, lat_local, first, heads, before=None):
    lat, columns = q.shape
    tall = (first + heads) * lat_local + LSE_ROWS
    block = min(ROW_BLOCK, lat)
    extra = () if before is None else (before,)
    return pl.pallas_call(
        functools.partial(cross_kernel, lat_local=lat_local, first=first, heads=heads),
        out_shape=jax.ShapeDtypeStruct((lat // lat_local, tall, HEAD_DIM), BF16),
        grid_spec=pltpu.PrefetchScalarGridSpec(
            num_scalar_prefetch=1,
            grid=(lat // block,),
            in_specs=[
                pl.BlockSpec((block, columns), lambda i, c: (i, 0)),
                full_spec(k),
                full_spec(v),
                *[pl.BlockSpec((block // lat_local,) + x.shape[1:], lambda i, c: (i, 0, 0)) for x in extra],
            ],
            out_specs=pl.BlockSpec((block // lat_local, tall, HEAD_DIM), lambda i, c: (i, 0, 0)),
            scratch_shapes=[pltpu.VMEM((2, block, k.shape[0]), F32)],
        ),
        compiler_params=params(32 << 20),
        cost_estimate=pl.CostEstimate(
            flops=4 * lat * k.shape[0] * heads * HEAD_DIM,
            bytes_accessed=4 << 20,
            transcendentals=lat * k.shape[0] * heads,
        ),
        name="cross",
    )(valid, q, k, v, *extra)


def in_hbm(*arrays):
    return [pltpu.with_memory_space_constraint(x, pltpu.HBM) for x in arrays]


def load(arrays):
    return pl.pallas_call(
        load_kernel,
        out_shape=[jax.ShapeDtypeStruct(x.shape, x.dtype) for x in arrays],
        in_specs=[pl.BlockSpec(memory_space=pltpu.HBM)] * len(arrays),
        out_specs=[pl.BlockSpec(memory_space=pltpu.VMEM)] * len(arrays),
        scratch_shapes=[pltpu.SemaphoreType.DMA((len(arrays),))],
        compiler_params=params(8 << 20),
        name="load",
    )(*in_hbm(*arrays))


def join(parts, lat_local):
    vmem = pl.BlockSpec(memory_space=pltpu.VMEM)
    return pl.pallas_call(
        functools.partial(join_kernel, lat_local=lat_local),
        out_shape=jax.ShapeDtypeStruct(parts[0].shape, BF16),
        in_specs=[vmem] * len(parts),
        out_specs=vmem,
        compiler_params=params(24 << 20),
        name="join",
    )(*parts)


def combine(core, gathered, w_out, w_mlp, lat_local):
    width = w_out.shape[1]
    half = lat_local // 2
    vmem = pl.BlockSpec(memory_space=pltpu.VMEM)
    hbm = pl.BlockSpec(memory_space=pltpu.HBM)
    return pl.pallas_call(
        functools.partial(combine_kernel, lat_local=lat_local),
        out_shape=(
            jax.ShapeDtypeStruct((half, width), F32),
            jax.ShapeDtypeStruct((half, width), BF16),
            jax.ShapeDtypeStruct(w_mlp.shape, BF16),
        ),
        in_specs=[pl.BlockSpec(memory_space=pltpu.SMEM), vmem, hbm, hbm],
        out_specs=(vmem, vmem, vmem),
        scratch_shapes=[
            pltpu.VMEM((2, half, width), F32),
            pltpu.VMEM((HEAD_DIM, gathered.shape[0] * (w_out.shape[0] // HEAD_DIM)), F32),
            pltpu.VMEM(w_out.shape, BF16),
            pltpu.SemaphoreType.DMA((2,)),
        ],
        compiler_params=params(24 << 20),
        name="combine",
    )(core, gathered, *in_hbm(w_out, w_mlp))


def spread(latents, w_query, devices):
    hbm = pl.BlockSpec(memory_space=pltpu.HBM)
    return pl.pallas_call(
        spread_kernel,
        out_shape=jax.ShapeDtypeStruct((devices, latents.shape[0], w_query.shape[1]), BF16),
        in_specs=[hbm, hbm],
        out_specs=pl.BlockSpec(memory_space=pltpu.VMEM),
        scratch_shapes=[
            pltpu.VMEM(latents.shape, BF16),
            pltpu.VMEM(w_query.shape, BF16),
            pltpu.SemaphoreType.DMA((2,)),
        ],
        compiler_params=params(60 << 20),
        name="spread",
    )(*in_hbm(latents, w_query))


def latent_rows(own, recv, w_mlp, devices):
    vmem = pl.BlockSpec(memory_space=pltpu.VMEM)
    return pl.pallas_call(
        latent_kernel,
        out_shape=jax.ShapeDtypeStruct((devices,) + own.shape, BF16),
        in_specs=[vmem] * 3,
        out_specs=vmem,
        compiler_params=params(24 << 20),
        name="latent",
    )(own, recv, w_mlp)


def latent_kv(rows, w_lkey, w_lvalue):
    vmem = pl.BlockSpec(memory_space=pltpu.VMEM)
    total = sum(r.shape[0] for r in rows)
    wide = w_lkey.shape[1] * 2
    return pl.pallas_call(
        kv_kernel,
        out_shape=jax.ShapeDtypeStruct((total, wide), BF16),
        in_specs=[vmem] * (len(rows) + 2),
        out_specs=vmem,
        compiler_params=params(24 << 20),
        cost_estimate=pl.CostEstimate(
            flops=2 * total * wide * w_lkey.shape[0], bytes_accessed=4 << 20, transcendentals=0
        ),
        name="latent_kv",
    )(*rows, w_lkey, w_lvalue)


def near_kv(near, swapped, w_lkey, w_lvalue, w_pout):
    vmem = pl.BlockSpec(memory_space=pltpu.VMEM)
    hbm = pl.BlockSpec(memory_space=pltpu.HBM)
    rows = near.shape[0] + swapped.shape[0]
    return pl.pallas_call(
        near_kv_kernel,
        out_shape=[
            jax.ShapeDtypeStruct((rows, 2 * w_lkey.shape[1]), BF16),
            *[jax.ShapeDtypeStruct(w.shape, BF16) for w in (w_lkey, w_lvalue, w_pout)],
        ],
        in_specs=[vmem, vmem, hbm, hbm, hbm],
        out_specs=[vmem] * 4,
        scratch_shapes=[pltpu.SemaphoreType.DMA((3,))],
        compiler_params=params(24 << 20),
        cost_estimate=pl.CostEstimate(
            flops=4 * rows * w_lkey.size // 2, bytes_accessed=4 << 20, transcendentals=0
        ),
        name="near_kv",
    )(near, swapped, *in_hbm(w_lkey, w_lvalue, w_pout))


def near_decode(q, kv):
    rows, columns = q.shape
    block = ROW_BLOCK
    return pl.pallas_call(
        near_kernel,
        out_shape=(
            jax.ShapeDtypeStruct((rows, columns), F32),
        )
        * 3,
        grid=(rows // block,),
        in_specs=[pl.BlockSpec((block, columns), lambda i: (i, 0)), full_spec(kv)],
        out_specs=(pl.BlockSpec((block, columns), lambda i: (i, 0)),) * 3,
        scratch_shapes=[pltpu.VMEM((2, block, kv.shape[0]), F32)],
        compiler_params=params(24 << 20),
        cost_estimate=pl.CostEstimate(
            flops=4 * rows * columns * kv.shape[0], bytes_accessed=4 << 20, transcendentals=4 * rows * kv.shape[0]
        ),
        name="near_decode",
    )(q, kv)


def decode(base, blocks, q, carried, kvs, w_pout, dtype, finish=()):
    columns = q.shape[1]
    width = w_pout.shape[1]
    block = ROW_BLOCK
    rows = blocks * block
    out_rows = finish[1].shape[0] if finish else rows
    out_block = out_rows if finish else block
    keys = sum(kv.shape[0] for kv in kvs)
    return pl.pallas_call(
        last_kernel if finish else decode_kernel,
        out_shape=jax.ShapeDtypeStruct((out_rows, width), dtype),
        grid_spec=pltpu.PrefetchScalarGridSpec(
            num_scalar_prefetch=1,
            grid=(blocks,),
            in_specs=[
                *[pl.BlockSpec((block, x.shape[1]), lambda i, b: (b[0] + i, 0)) for x in (q, *carried)],
                *[full_spec(x) for x in (*kvs, w_pout, *finish)],
            ],
            out_specs=pl.BlockSpec((out_block, width), lambda i, b: (i, 0)),
            scratch_shapes=[pltpu.VMEM((2, block, keys), F32), pltpu.VMEM((block, columns), BF16)],
        ),
        compiler_params=params(36 << 20),
        cost_estimate=pl.CostEstimate(
            flops=4 * rows * columns * keys, bytes_accessed=8 << 20, transcendentals=4 * rows * keys
        ),
        name="decode",
    )(base, q, *carried, *kvs, w_pout, *finish)


def project(a, w):
    return jnp.dot(a, w, preferred_element_type=F32).astype(BF16)


def per_device(
    inputs,
    valid_blocks,
    latents,
    w_query,
    w_key,
    w_value,
    w_out,
    w_mlp,
    w_lkey,
    w_lvalue,
    w_pquery,
    w_pout,
):
    lat_local = latents.shape[0]
    columns = w_key.shape[1]
    width = inputs.shape[1]
    core = lax.axis_index("head").astype(jnp.int32).reshape(1)
    swap = [(0, 1), (1, 0)]

    plane, long = plane_groups()

    def within_plane(x):
        return lax.all_to_all(x, AXES, 0, 0, axis_index_groups=plane)

    def along(x, shift):
        return lax.ppermute(x, AXES, long[shift % SIDE])

    queries = within_plane(spread(latents, w_query, SIDE * SIDE)).reshape(-1, columns)
    keys = project(inputs, w_key)
    values = project(inputs, w_value)
    queries, keys, values = lax.optimization_barrier((queries, keys, values))
    away = [along(queries, s) for s in ORDER]
    keys, values = load((keys, values))
    heads = columns // HEAD_DIM
    half = cross(valid_blocks, queries, keys, values, lat_local, 0, heads // 2)
    part, partials = half, []
    for s, there in zip(ORDER, away):
        part, there = lax.optimization_barrier((part, there))
        part = cross(valid_blocks, there, keys, values, lat_local, 0, heads)
        partials.append(along(part, -s))
    part, half = lax.optimization_barrier((part, half))
    partials.append(cross(valid_blocks, queries, keys, values, lat_local, heads // 2, heads // 2, half))
    gathered = within_plane(join(partials, lat_local))
    own, other, w_mlp = combine(jnp.concatenate([core, lane_offset(lat_local)]), gathered, w_out, w_mlp, lat_local)
    recv = lax.ppermute(other, "head", swap)
    rows = latent_rows(own, recv, w_mlp, SIDE * SIDE)
    rows, inputs = lax.optimization_barrier((rows, inputs))
    pos_queries = project(inputs, w_pquery)
    near, pos_queries = lax.optimization_barrier((within_plane(rows), pos_queries))
    near = near.reshape(-1, width)
    far = [along(near, s) for s in ORDER]
    kv, w_lkey, w_lvalue, w_pout = near_kv(near, lax.ppermute(near, "head", swap), w_lkey, w_lvalue, w_pout)
    carried = near_decode(pos_queries, kv)
    carried, far = lax.optimization_barrier((carried, far))
    far_swapped = [lax.ppermute(x, "head", swap) for x in far]
    kvs = [latent_kv(far, w_lkey, w_lvalue), latent_kv(far_swapped, w_lkey, w_lvalue)]
    blocks = pos_queries.shape[0] // 2 // ROW_BLOCK
    terms = decode((1 - core) * blocks, blocks, pos_queries, carried, kvs, w_pout, BF16)
    arrived = lax.ppermute(terms, "head", swap)
    first = decode(core * blocks, blocks - 1, pos_queries, carried, kvs, w_pout, F32)
    return decode(core * blocks + blocks - 1, 1, pos_queries, carried, kvs, w_pout, BF16, (first, arrived))


def solution(mesh):
    placed = (
        P("pos", None),
        P("pos"),
        P("pos", None),
        P(None, "head"),
        P(None, "head"),
        P(None, "head"),
        P("head", None),
        P(),
        P(None, "head"),
        P(None, "head"),
        P(None, "head"),
        P("head", None),
    )

    return jax.shard_map(
        per_device,
        mesh=mesh,
        in_specs=placed,
        out_specs=P(("pos", "head"), None),
        check_vma=False,
    )
```

```python
import functools

import jax
import jax.numpy as jnp
from jax import lax
from jax.experimental import pallas as pl
from jax.experimental.pallas import tpu as pltpu
from jax.sharding import PartitionSpec as P


HEAD_DIM = 128
BLK = 128
SCALE = HEAD_DIM ** (-0.5)
LOG2E = 1.4426950408889634
MASKED = -1e30
EPS = 1e-05
F32 = jnp.float32
BF16 = jnp.bfloat16
ROW_BLOCK = 256
LSE_ROWS = 16


AXES = ("pos", "head")
SIDE = 4
ORDER = (1, 2, 3)
FAR_ORDER = (2, 1, 3)


def plane_groups():
    def device(z, y, x, core):
        return ((z * SIDE + y) * SIDE + x) * 2 + core

    r = range(SIDE)
    plane = [[device(z, y, x, 0) for y in r for x in r] for z in r]
    plane += [[device(z, y, x, 1) for z in r for x in r] for y in r]
    long = {}
    for s in range(1, SIDE):
        long[s] = [
            pair
            for z in r
            for y in r
            for x in r
            for pair in (
                (device(z, y, x, 0), device((z + s) % SIDE, y, x, 0)),
                (device(z, y, x, 1), device(z, (y + s) % SIDE, x, 1)),
            )
        ]
    return plane, long


def lane_offset(lat_local):
    x = lax.axis_index("pos") % SIDE
    return (x % (HEAD_DIM // lat_local) * lat_local).astype(jnp.int32).reshape(1)


def rms_norm(values):
    return values * lax.rsqrt(jnp.mean(values * values, axis=-1, keepdims=True) + EPS)


def nt_dot(a, b):
    return lax.dot_general(a, b, (((1,), (1,)), ((), ())), preferred_element_type=F32)


def bf16_pieces(x):
    hi = x.astype(BF16).astype(F32)
    mid = (x - hi).astype(BF16).astype(F32)
    low = (x - hi - mid).astype(BF16).astype(F32)
    return hi, mid, low


def pack_rows(lse, heads):
    rows = jnp.concatenate([p[:heads] for p in bf16_pieces(lse)], axis=0)
    pad = jnp.zeros((LSE_ROWS - rows.shape[0], rows.shape[1]), F32)
    return jnp.concatenate([rows, pad], axis=0).astype(BF16)


def unpack_rows(packed, heads):
    x = packed.astype(F32)
    return x[:heads] + x[heads : 2 * heads] + x[2 * heads : 3 * heads]


def pipelined(count, score, use):
    score(0)
    for i in range(count):
        if i + 1 < count:
            score(i + 1)
        use(i)


def cross_kernel(valid_ref, q_ref, k_ref, v_ref, *refs, lat_local, first, heads):
    *before, out_ref, s_ref = refs
    rows = q_ref.shape[0]
    owners = rows // lat_local
    all_heads = q_ref.shape[1] // HEAD_DIM
    done = first * lat_local
    span = done + heads * lat_local
    keys = k_ref.shape[0]
    valid = sum(valid_ref[i] for i in range(keys // BLK)) * BLK
    live = lax.broadcasted_iota(jnp.int32, (1, keys), 1) < valid
    bias = jnp.where(live, 0.0, MASKED)
    lane = lax.broadcasted_iota(jnp.int32, (rows, HEAD_DIM), 1)
    if before:
        out_ref[:, :done, :] = before[0][:, :done, :]
    tops = jnp.zeros((rows, HEAD_DIM), F32)
    totals = jnp.ones((rows, HEAD_DIM), F32)

    def columns(i):
        return slice((first + i) * HEAD_DIM, (first + i + 1) * HEAD_DIM)

    def score(i):
        s_ref[i % 2] = nt_dot(q_ref[:, columns(i)], k_ref[:, columns(i)]) + bias

    def use(i):
        nonlocal tops, totals
        s = s_ref[i % 2]
        m = jnp.max(s, axis=1, keepdims=True)
        p = jnp.exp2((s - m) * (SCALE * LOG2E))
        total = jnp.sum(p, axis=1, keepdims=True)
        o = jnp.dot(p.astype(BF16), v_ref[:, columns(i)], preferred_element_type=F32)
        o = (o / total).astype(BF16)
        top = (first + i) * lat_local
        out_ref[:, top : top + lat_local, :] = o.reshape(owners, lat_local, HEAD_DIM)
        mine = lane % all_heads == first + i
        tops = jnp.where(mine, m, tops)
        totals = jnp.where(mine, total, totals)

    pipelined(heads, score, use)
    hi, mid, low = bf16_pieces(tops * SCALE + jnp.log(totals))
    place = lane // all_heads
    packed = jnp.where(place == 0, hi, jnp.where(place == 1, mid, jnp.where(place == 2, low, 0.0)))
    eye = lax.broadcasted_iota(jnp.int32, (LSE_ROWS, HEAD_DIM), 0)
    eye = (eye == lax.broadcasted_iota(jnp.int32, (LSE_ROWS, HEAD_DIM), 1)).astype(BF16)
    turned = nt_dot(eye, packed.astype(BF16)).astype(BF16)
    for d in range(owners):
        at = d * lat_local // HEAD_DIM * HEAD_DIM
        rows_d = turned[:, at : at + HEAD_DIM]
        if before:
            rows_d = rows_d + before[0][d, done : done + LSE_ROWS, :]
        out_ref[d, span : span + LSE_ROWS, :] = rows_d


def load_kernel(*refs):
    n = len(refs) // 2
    *pairs, sems = refs
    copies = [pltpu.make_async_copy(pairs[i], pairs[n + i], sems.at[i]) for i in range(n)]
    for copy in copies:
        copy.start()
    for copy in copies:
        copy.wait()


def join_kernel(*refs, lat_local):
    *parts, out_ref = refs
    owners, tall, _ = out_ref.shape
    span = tall - LSE_ROWS
    heads = span // lat_local
    group = HEAD_DIM // lat_local
    for g in range(0, owners, group):
        lses = [unpack_rows(r[g, span : span + LSE_ROWS, :], heads) for r in parts]
        top = functools.reduce(jnp.maximum, lses)
        ws = [jnp.exp(x - top) for x in lses]
        total = functools.reduce(jnp.add, ws)
        packed = pack_rows(top + jnp.log(total), heads)
        stacked = jnp.concatenate([w / total for w in ws], axis=0)
        wt = jnp.transpose(stacked)
        for d in range(group):
            out_ref[g + d, span : span + LSE_ROWS, :] = packed
            for h in range(heads):
                rows = slice(h * lat_local, (h + 1) * lat_local)
                acc = jnp.zeros((lat_local, HEAD_DIM), F32)
                for i, r in enumerate(parts):
                    w = wt[d * lat_local : (d + 1) * lat_local, i * heads + h : i * heads + h + 1]
                    acc = acc + w * r[g + d, rows, :].astype(F32)
                out_ref[g + d, rows, :] = acc.astype(BF16)


def combine_kernel(core_ref, r_ref, w_ref, mlp_ref, own_ref, other_ref, mlp_out, terms_ref, spot_ref, w_vmem, sems, *, lat_local):
    copies = [
        pltpu.make_async_copy(w_ref, w_vmem, sems.at[0]),
        pltpu.make_async_copy(mlp_ref, mlp_out, sems.at[1]),
    ]
    for copy in copies:
        copy.start()
    devices, tall, _ = r_ref.shape
    span = tall - LSE_ROWS
    heads = span // lat_local
    lses = [unpack_rows(r_ref[d, span : span + LSE_ROWS, :], heads) for d in range(devices)]
    top = functools.reduce(jnp.maximum, lses)
    ws = [jnp.exp(x - top) for x in lses]
    total = functools.reduce(jnp.add, ws)
    stacked = jnp.concatenate([w / total for w in ws], axis=0)
    spot_ref[...] = jnp.transpose(stacked)
    wt = spot_ref[pl.ds(pl.multiple_of(core_ref[1], lat_local), lat_local), :]
    parts = []
    for h in range(heads):
        acc = jnp.zeros((lat_local, HEAD_DIM), F32)
        for d in range(devices):
            w = wt[:, d * heads + h : d * heads + h + 1]
            acc = acc + w * r_ref[d, h * lat_local : (h + 1) * lat_local, :].astype(F32)
        parts.append(acc.astype(BF16))
    copies[0].wait()
    terms = jnp.zeros((lat_local, w_vmem.shape[1]), F32)
    for h in range(span // lat_local):
        terms = terms + jnp.dot(
            parts[h],
            w_vmem[h * HEAD_DIM : (h + 1) * HEAD_DIM, :],
            preferred_element_type=F32,
        )
    half = lat_local // 2
    terms_ref[...] = terms.reshape(2, half, w_vmem.shape[1])
    own_ref[...] = terms_ref[core_ref[0]]
    other_ref[...] = terms_ref[1 - core_ref[0]].astype(BF16)
    copies[1].wait()


def spread_kernel(l_ref, w_ref, out_ref, l_vmem, w_vmem, sems):
    copies = [
        pltpu.make_async_copy(w_ref, w_vmem, sems.at[0]),
        pltpu.make_async_copy(l_ref, l_vmem, sems.at[1]),
    ]
    for copy in copies:
        copy.start()
    for copy in copies:
        copy.wait()
    q = jnp.dot(l_vmem[...], w_vmem[...], preferred_element_type=F32).astype(BF16)
    out_ref[...] = jnp.broadcast_to(q[None], out_ref.shape)


def latent_kernel(own_ref, recv_ref, w_ref, out_ref):
    normed = rms_norm(own_ref[...] + recv_ref[...].astype(F32))
    hidden = jax.nn.gelu(jnp.dot(normed.astype(BF16), w_ref[...], preferred_element_type=F32))
    rows = (normed + hidden).astype(BF16)
    out_ref[...] = jnp.broadcast_to(rows[None], out_ref.shape)


def write_kv(row_refs, w_ref, out_ref, first):
    at = 0
    wide = w_ref.shape[1]
    for r in row_refs:
        n = r.shape[0]
        out_ref[at : at + n, first : first + wide] = jnp.dot(
            r[...], w_ref[...], preferred_element_type=F32
        ).astype(BF16)
        at += n


def kv_kernel(*refs):
    *row_refs, k_ref, v_ref, out_ref = refs
    write_kv(row_refs, k_ref, out_ref, 0)
    write_kv(row_refs, v_ref, out_ref, k_ref.shape[1])


def near_kv_kernel(near_ref, swapped_ref, k_ref, v_ref, p_ref, out_ref, k_out, v_out, p_out, sems):
    pairs = ((k_ref, k_out), (v_ref, v_out), (p_ref, p_out))
    copies = [pltpu.make_async_copy(a, b, sems.at[i]) for i, (a, b) in enumerate(pairs)]
    for copy in copies:
        copy.start()
    rows = (near_ref, swapped_ref)
    copies[0].wait()
    write_kv(rows, k_out, out_ref, 0)
    copies[1].wait()
    write_kv(rows, v_out, out_ref, k_out.shape[1])
    copies[2].wait()


def head_columns(columns, h):
    return (
        slice(h * HEAD_DIM, (h + 1) * HEAD_DIM),
        slice(columns + h * HEAD_DIM, columns + (h + 1) * HEAD_DIM),
    )


def near_kernel(q_ref, kv_ref, sums_ref, tops_ref, totals_ref, s_ref):
    columns = q_ref.shape[1]
    shape = (q_ref.shape[0], HEAD_DIM)

    def score(h):
        kc, _ = head_columns(columns, h)
        s_ref[h % 2] = nt_dot(q_ref[:, kc], kv_ref[:, kc])

    def use(h):
        kc, vc = head_columns(columns, h)
        s = s_ref[h % 2]
        m = jnp.max(s, axis=1, keepdims=True)
        p = jnp.exp2((s - m) * (SCALE * LOG2E))
        sums_ref[:, kc] = jnp.dot(p.astype(BF16), kv_ref[:, vc], preferred_element_type=F32)
        tops_ref[:, kc] = jnp.broadcast_to(m, shape)
        totals_ref[:, kc] = jnp.broadcast_to(jnp.sum(p, axis=1, keepdims=True), shape)

    pipelined(columns // HEAD_DIM, score, use)


def attend(q_ref, carried_refs, kv_refs, w_ref, s_ref, o_ref):
    sums_ref, tops_ref, totals_ref = carried_refs
    columns = q_ref.shape[1]
    spots = []
    at = 0
    for kv in kv_refs:
        spots.append(slice(at, at + kv.shape[0]))
        at += kv.shape[0]

    def score(h):
        kc, _ = head_columns(columns, h)
        for spot, kv in zip(spots, kv_refs):
            s_ref[h % 2, :, spot] = nt_dot(q_ref[:, kc], kv[:, kc])

    def use(h):
        kc, vc = head_columns(columns, h)
        s = s_ref[h % 2]
        before = tops_ref[:, kc]
        m = jnp.maximum(before, jnp.max(s, axis=1, keepdims=True))
        keep = jnp.exp2((before - m) * (SCALE * LOG2E))
        p = jnp.exp2((s - m[:, :1]) * (SCALE * LOG2E))
        total = totals_ref[:, kc] * keep + jnp.sum(p, axis=1, keepdims=True)
        o = sums_ref[:, kc] * keep
        pb = p.astype(BF16)
        for spot, kv in zip(spots, kv_refs):
            o = o + jnp.dot(pb[:, spot], kv[:, vc], preferred_element_type=F32)
        o_ref[:, kc] = (o / total).astype(BF16)

    pipelined(columns // HEAD_DIM, score, use)
    return jnp.dot(o_ref[...], w_ref[...], preferred_element_type=F32)


def decode_kernel(base_ref, q_ref, *refs):
    carried, (*kv_refs, w_ref, out_ref, s_ref, o_ref) = refs[:3], refs[3:]
    out_ref[...] = attend(q_ref, carried, kv_refs, w_ref, s_ref, o_ref).astype(out_ref.dtype)


def last_kernel(base_ref, q_ref, *refs):
    carried, (*kv_refs, w_ref, first_ref, recv_ref, out_ref, s_ref, o_ref) = refs[:3], refs[3:]
    n = first_ref.shape[0]
    out_ref[:n] = rms_norm(first_ref[...] + recv_ref[:n].astype(F32)).astype(out_ref.dtype)
    terms = attend(q_ref, carried, kv_refs, w_ref, s_ref, o_ref)
    out_ref[n:] = rms_norm(terms + recv_ref[n:].astype(F32)).astype(out_ref.dtype)


def full_spec(array):
    return pl.BlockSpec(array.shape, lambda *_: (0,) * array.ndim)


def params(limit=56 << 20):
    return pltpu.CompilerParams(vmem_limit_bytes=limit)


def cross(valid, q, k, v, lat_local, first, heads, before=None):
    lat, columns = q.shape
    tall = (first + heads) * lat_local + LSE_ROWS
    block = min(ROW_BLOCK, lat)
    extra = () if before is None else (before,)
    return pl.pallas_call(
        functools.partial(cross_kernel, lat_local=lat_local, first=first, heads=heads),
        out_shape=jax.ShapeDtypeStruct((lat // lat_local, tall, HEAD_DIM), BF16),
        grid_spec=pltpu.PrefetchScalarGridSpec(
            num_scalar_prefetch=1,
            grid=(lat // block,),
            in_specs=[
                pl.BlockSpec((block, columns), lambda i, c: (i, 0)),
                full_spec(k),
                full_spec(v),
                *[pl.BlockSpec((block // lat_local,) + x.shape[1:], lambda i, c: (i, 0, 0)) for x in extra],
            ],
            out_specs=pl.BlockSpec((block // lat_local, tall, HEAD_DIM), lambda i, c: (i, 0, 0)),
            scratch_shapes=[pltpu.VMEM((2, block, k.shape[0]), F32)],
        ),
        compiler_params=params(32 << 20),
        cost_estimate=pl.CostEstimate(
            flops=4 * lat * k.shape[0] * heads * HEAD_DIM,
            bytes_accessed=4 << 20,
            transcendentals=lat * k.shape[0] * heads,
        ),
        name="cross",
    )(valid, q, k, v, *extra)


def in_hbm(*arrays):
    return [pltpu.with_memory_space_constraint(x, pltpu.HBM) for x in arrays]


def load(arrays):
    return pl.pallas_call(
        load_kernel,
        out_shape=[jax.ShapeDtypeStruct(x.shape, x.dtype) for x in arrays],
        in_specs=[pl.BlockSpec(memory_space=pltpu.HBM)] * len(arrays),
        out_specs=[pl.BlockSpec(memory_space=pltpu.VMEM)] * len(arrays),
        scratch_shapes=[pltpu.SemaphoreType.DMA((len(arrays),))],
        compiler_params=params(8 << 20),
        name="load",
    )(*in_hbm(*arrays))


def join(parts, lat_local):
    vmem = pl.BlockSpec(memory_space=pltpu.VMEM)
    return pl.pallas_call(
        functools.partial(join_kernel, lat_local=lat_local),
        out_shape=jax.ShapeDtypeStruct(parts[0].shape, BF16),
        in_specs=[vmem] * len(parts),
        out_specs=vmem,
        compiler_params=params(24 << 20),
        name="join",
    )(*parts)


def combine(core, gathered, w_out, w_mlp, lat_local):
    width = w_out.shape[1]
    half = lat_local // 2
    vmem = pl.BlockSpec(memory_space=pltpu.VMEM)
    hbm = pl.BlockSpec(memory_space=pltpu.HBM)
    return pl.pallas_call(
        functools.partial(combine_kernel, lat_local=lat_local),
        out_shape=(
            jax.ShapeDtypeStruct((half, width), F32),
            jax.ShapeDtypeStruct((half, width), BF16),
            jax.ShapeDtypeStruct(w_mlp.shape, BF16),
        ),
        in_specs=[pl.BlockSpec(memory_space=pltpu.SMEM), vmem, hbm, hbm],
        out_specs=(vmem, vmem, vmem),
        scratch_shapes=[
            pltpu.VMEM((2, half, width), F32),
            pltpu.VMEM((HEAD_DIM, gathered.shape[0] * (w_out.shape[0] // HEAD_DIM)), F32),
            pltpu.VMEM(w_out.shape, BF16),
            pltpu.SemaphoreType.DMA((2,)),
        ],
        compiler_params=params(24 << 20),
        name="combine",
    )(core, gathered, *in_hbm(w_out, w_mlp))


def spread(latents, w_query, devices):
    hbm = pl.BlockSpec(memory_space=pltpu.HBM)
    return pl.pallas_call(
        spread_kernel,
        out_shape=jax.ShapeDtypeStruct((devices, latents.shape[0], w_query.shape[1]), BF16),
        in_specs=[hbm, hbm],
        out_specs=pl.BlockSpec(memory_space=pltpu.VMEM),
        scratch_shapes=[
            pltpu.VMEM(latents.shape, BF16),
            pltpu.VMEM(w_query.shape, BF16),
            pltpu.SemaphoreType.DMA((2,)),
        ],
        compiler_params=params(60 << 20),
        name="spread",
    )(*in_hbm(latents, w_query))


def latent_rows(own, recv, w_mlp, devices):
    vmem = pl.BlockSpec(memory_space=pltpu.VMEM)
    return pl.pallas_call(
        latent_kernel,
        out_shape=jax.ShapeDtypeStruct((devices,) + own.shape, BF16),
        in_specs=[vmem] * 3,
        out_specs=vmem,
        compiler_params=params(24 << 20),
        name="latent",
    )(own, recv, w_mlp)


def latent_kv(rows, w_lkey, w_lvalue):
    vmem = pl.BlockSpec(memory_space=pltpu.VMEM)
    total = sum(r.shape[0] for r in rows)
    wide = w_lkey.shape[1] * 2
    return pl.pallas_call(
        kv_kernel,
        out_shape=jax.ShapeDtypeStruct((total, wide), BF16),
        in_specs=[vmem] * (len(rows) + 2),
        out_specs=vmem,
        compiler_params=params(24 << 20),
        cost_estimate=pl.CostEstimate(
            flops=2 * total * wide * w_lkey.shape[0], bytes_accessed=4 << 20, transcendentals=0
        ),
        name="latent_kv",
    )(*rows, w_lkey, w_lvalue)


def near_kv(near, swapped, w_lkey, w_lvalue, w_pout):
    vmem = pl.BlockSpec(memory_space=pltpu.VMEM)
    hbm = pl.BlockSpec(memory_space=pltpu.HBM)
    rows = near.shape[0] + swapped.shape[0]
    return pl.pallas_call(
        near_kv_kernel,
        out_shape=[
            jax.ShapeDtypeStruct((rows, 2 * w_lkey.shape[1]), BF16),
            *[jax.ShapeDtypeStruct(w.shape, BF16) for w in (w_lkey, w_lvalue, w_pout)],
        ],
        in_specs=[vmem, vmem, hbm, hbm, hbm],
        out_specs=[vmem] * 4,
        scratch_shapes=[pltpu.SemaphoreType.DMA((3,))],
        compiler_params=params(24 << 20),
        cost_estimate=pl.CostEstimate(
            flops=4 * rows * w_lkey.size // 2, bytes_accessed=4 << 20, transcendentals=0
        ),
        name="near_kv",
    )(near, swapped, *in_hbm(w_lkey, w_lvalue, w_pout))


def near_decode(q, kv):
    rows, columns = q.shape
    block = ROW_BLOCK
    return pl.pallas_call(
        near_kernel,
        out_shape=(
            jax.ShapeDtypeStruct((rows, columns), F32),
        )
        * 3,
        grid=(rows // block,),
        in_specs=[pl.BlockSpec((block, columns), lambda i: (i, 0)), full_spec(kv)],
        out_specs=(pl.BlockSpec((block, columns), lambda i: (i, 0)),) * 3,
        scratch_shapes=[pltpu.VMEM((2, block, kv.shape[0]), F32)],
        compiler_params=params(24 << 20),
        cost_estimate=pl.CostEstimate(
            flops=4 * rows * columns * kv.shape[0], bytes_accessed=4 << 20, transcendentals=4 * rows * kv.shape[0]
        ),
        name="near_decode",
    )(q, kv)


def decode(base, blocks, q, carried, kvs, w_pout, dtype, finish=()):
    columns = q.shape[1]
    width = w_pout.shape[1]
    block = ROW_BLOCK
    rows = blocks * block
    out_rows = finish[1].shape[0] if finish else rows
    out_block = out_rows if finish else block
    keys = sum(kv.shape[0] for kv in kvs)
    return pl.pallas_call(
        last_kernel if finish else decode_kernel,
        out_shape=jax.ShapeDtypeStruct((out_rows, width), dtype),
        grid_spec=pltpu.PrefetchScalarGridSpec(
            num_scalar_prefetch=1,
            grid=(blocks,),
            in_specs=[
                *[pl.BlockSpec((block, x.shape[1]), lambda i, b: (b[0] + i, 0)) for x in (q, *carried)],
                *[full_spec(x) for x in (*kvs, w_pout, *finish)],
            ],
            out_specs=pl.BlockSpec((out_block, width), lambda i, b: (i, 0)),
            scratch_shapes=[pltpu.VMEM((2, block, keys), F32), pltpu.VMEM((block, columns), BF16)],
        ),
        compiler_params=params(36 << 20),
        cost_estimate=pl.CostEstimate(
            flops=4 * rows * columns * keys, bytes_accessed=8 << 20, transcendentals=4 * rows * keys
        ),
        name="decode",
    )(base, q, *carried, *kvs, w_pout, *finish)


def project(a, w):
    return jnp.dot(a, w, preferred_element_type=F32).astype(BF16)


def per_device(
    inputs,
    valid_blocks,
    latents,
    w_query,
    w_key,
    w_value,
    w_out,
    w_mlp,
    w_lkey,
    w_lvalue,
    w_pquery,
    w_pout,
):
    lat_local = latents.shape[0]
    columns = w_key.shape[1]
    width = inputs.shape[1]
    core = lax.axis_index("head").astype(jnp.int32).reshape(1)
    swap = [(0, 1), (1, 0)]

    plane, long = plane_groups()

    def within_plane(x):
        return lax.all_to_all(x, AXES, 0, 0, axis_index_groups=plane)

    def along(x, shift):
        return lax.ppermute(x, AXES, long[shift % SIDE])

    queries = within_plane(spread(latents, w_query, SIDE * SIDE)).reshape(-1, columns)
    keys = project(inputs, w_key)
    values = project(inputs, w_value)
    queries, keys, values = lax.optimization_barrier((queries, keys, values))
    away = [along(queries, s) for s in ORDER]
    keys, values = load((keys, values))
    heads = columns // HEAD_DIM
    half = cross(valid_blocks, queries, keys, values, lat_local, 0, heads // 2)
    part, partials = half, []
    for s, there in zip(ORDER, away):
        part, there = lax.optimization_barrier((part, there))
        part = cross(valid_blocks, there, keys, values, lat_local, 0, heads)
        partials.append(along(part, -s))
    part, half = lax.optimization_barrier((part, half))
    stay = cross(valid_blocks, queries, keys, values, lat_local, heads // 2, heads // 2, half)
    *early, late = partials
    stay, late = lax.optimization_barrier((join([stay, *early], lat_local), late))
    partials = [stay, late]
    gathered = within_plane(join(partials, lat_local))
    own, other, w_mlp = combine(jnp.concatenate([core, lane_offset(lat_local)]), gathered, w_out, w_mlp, lat_local)
    recv = lax.ppermute(other, "head", swap)
    rows = latent_rows(own, recv, w_mlp, SIDE * SIDE)
    rows, inputs = lax.optimization_barrier((rows, inputs))
    pos_queries = project(inputs, w_pquery)
    near, pos_queries = lax.optimization_barrier((within_plane(rows), pos_queries))
    near = near.reshape(-1, width)
    far = []
    for s in FAR_ORDER:
        far.append(along(near, s))
    near_swapped = lax.ppermute(near, "head", swap)
    kv, w_lkey, w_lvalue, w_pout = near_kv(near, near_swapped, w_lkey, w_lvalue, w_pout)
    carried = near_decode(pos_queries, kv)
    slow, *quick = far
    carried, quick = lax.optimization_barrier((carried, quick))
    quick_swapped = [lax.ppermute(x, "head", swap) for x in quick]
    quick_kv = latent_kv(quick, w_lkey, w_lvalue)
    slow, quick_kv = lax.optimization_barrier((slow, quick_kv))
    slow_swapped = lax.ppermute(slow, "head", swap)
    swapped_kv = latent_kv(quick_swapped, w_lkey, w_lvalue)
    slow_kv = latent_kv([slow, slow_swapped], w_lkey, w_lvalue)
    kvs = [quick_kv, swapped_kv, slow_kv]
    blocks = pos_queries.shape[0] // 2 // ROW_BLOCK
    terms = decode((1 - core) * blocks, blocks, pos_queries, carried, kvs, w_pout, BF16)
    arrived = lax.ppermute(terms, "head", swap)
    first = decode(core * blocks, blocks - 1, pos_queries, carried, kvs, w_pout, F32)
    return decode(core * blocks + blocks - 1, 1, pos_queries, carried, kvs, w_pout, BF16, (first, arrived))


def solution(mesh):
    placed = (
        P("pos", None),
        P("pos"),
        P("pos", None),
        P(None, "head"),
        P(None, "head"),
        P(None, "head"),
        P("head", None),
        P(),
        P(None, "head"),
        P(None, "head"),
        P(None, "head"),
        P("head", None),
    )

    return jax.shard_map(
        per_device,
        mesh=mesh,
        in_specs=placed,
        out_specs=P(("pos", "head"), None),
        check_vma=False,
    )
```

```python
import functools

import jax
import jax.numpy as jnp
from jax import lax
from jax.experimental import pallas as pl
from jax.experimental.pallas import tpu as pltpu
from jax.sharding import PartitionSpec as P


HEAD_DIM = 128
BLK = 128
SCALE = HEAD_DIM ** (-0.5)
LOG2E = 1.4426950408889634
MASKED = -1e30
EPS = 1e-05
F32 = jnp.float32
BF16 = jnp.bfloat16
ROW_BLOCK = 256
LSE_ROWS = 16


AXES = ("pos", "head")
SIDE = 4
ORDER = (1, 2, 3)


def plane_groups():
    def device(z, y, x, core):
        return ((z * SIDE + y) * SIDE + x) * 2 + core

    r = range(SIDE)
    plane = [[device(z, y, x, 0) for y in r for x in r] for z in r]
    plane += [[device(z, y, x, 1) for z in r for x in r] for y in r]
    long = {}
    for s in range(1, SIDE):
        long[s] = [
            pair
            for z in r
            for y in r
            for x in r
            for pair in (
                (device(z, y, x, 0), device((z + s) % SIDE, y, x, 0)),
                (device(z, y, x, 1), device(z, (y + s) % SIDE, x, 1)),
            )
        ]
    return plane, long


def lane_offset(lat_local):
    x = lax.axis_index("pos") % SIDE
    return (x % (HEAD_DIM // lat_local) * lat_local).astype(jnp.int32).reshape(1)


def rms_norm(values):
    return values * lax.rsqrt(jnp.mean(values * values, axis=-1, keepdims=True) + EPS)


def nt_dot(a, b):
    return lax.dot_general(a, b, (((1,), (1,)), ((), ())), preferred_element_type=F32)


def bf16_pieces(x):
    hi = x.astype(BF16).astype(F32)
    mid = (x - hi).astype(BF16).astype(F32)
    low = (x - hi - mid).astype(BF16).astype(F32)
    return hi, mid, low


def pack_rows(lse, heads):
    rows = jnp.concatenate([p[:heads] for p in bf16_pieces(lse)], axis=0)
    pad = jnp.zeros((LSE_ROWS - rows.shape[0], rows.shape[1]), F32)
    return jnp.concatenate([rows, pad], axis=0).astype(BF16)


def unpack_rows(packed, heads):
    x = packed.astype(F32)
    return x[:heads] + x[heads : 2 * heads] + x[2 * heads : 3 * heads]


def pipelined(count, score, use):
    score(0)
    for i in range(count):
        if i + 1 < count:
            score(i + 1)
        use(i)


def cross_kernel(valid_ref, q_ref, k_ref, v_ref, *refs, lat_local, first, heads):
    *before, out_ref, s_ref = refs
    rows = q_ref.shape[0]
    owners = rows // lat_local
    all_heads = q_ref.shape[1] // HEAD_DIM
    done = first * lat_local
    span = done + heads * lat_local
    keys = k_ref.shape[0]
    valid = sum(valid_ref[i] for i in range(keys // BLK)) * BLK
    live = lax.broadcasted_iota(jnp.int32, (1, keys), 1) < valid
    bias = jnp.where(live, 0.0, MASKED)
    lane = lax.broadcasted_iota(jnp.int32, (rows, HEAD_DIM), 1)
    if before:
        out_ref[:, :done, :] = before[0][:, :done, :]
    tops = jnp.zeros((rows, HEAD_DIM), F32)
    totals = jnp.ones((rows, HEAD_DIM), F32)

    def columns(i):
        return slice((first + i) * HEAD_DIM, (first + i + 1) * HEAD_DIM)

    def score(i):
        s_ref[i % 2] = nt_dot(q_ref[:, columns(i)], k_ref[:, columns(i)]) + bias

    def use(i):
        nonlocal tops, totals
        s = s_ref[i % 2]
        m = jnp.max(s, axis=1, keepdims=True)
        p = jnp.exp2((s - m) * (SCALE * LOG2E))
        total = jnp.sum(p, axis=1, keepdims=True)
        o = jnp.dot(p.astype(BF16), v_ref[:, columns(i)], preferred_element_type=F32)
        o = (o / total).astype(BF16)
        top = (first + i) * lat_local
        out_ref[:, top : top + lat_local, :] = o.reshape(owners, lat_local, HEAD_DIM)
        mine = lane % all_heads == first + i
        tops = jnp.where(mine, m, tops)
        totals = jnp.where(mine, total, totals)

    pipelined(heads, score, use)
    hi, mid, low = bf16_pieces(tops * SCALE + jnp.log(totals))
    place = lane // all_heads
    packed = jnp.where(place == 0, hi, jnp.where(place == 1, mid, jnp.where(place == 2, low, 0.0)))
    eye = lax.broadcasted_iota(jnp.int32, (LSE_ROWS, HEAD_DIM), 0)
    eye = (eye == lax.broadcasted_iota(jnp.int32, (LSE_ROWS, HEAD_DIM), 1)).astype(BF16)
    turned = nt_dot(eye, packed.astype(BF16)).astype(BF16)
    for d in range(owners):
        at = d * lat_local // HEAD_DIM * HEAD_DIM
        rows_d = turned[:, at : at + HEAD_DIM]
        if before:
            rows_d = rows_d + before[0][d, done : done + LSE_ROWS, :]
        out_ref[d, span : span + LSE_ROWS, :] = rows_d


def load_kernel(*refs):
    n = len(refs) // 2
    *pairs, sems = refs
    copies = [pltpu.make_async_copy(pairs[i], pairs[n + i], sems.at[i]) for i in range(n)]
    for copy in copies:
        copy.start()
    for copy in copies:
        copy.wait()


def join_kernel(*refs, lat_local):
    *parts, out_ref = refs
    owners, tall, _ = out_ref.shape
    span = tall - LSE_ROWS
    heads = span // lat_local
    group = HEAD_DIM // lat_local
    for g in range(0, owners, group):
        lses = [unpack_rows(r[g, span : span + LSE_ROWS, :], heads) for r in parts]
        top = functools.reduce(jnp.maximum, lses)
        ws = [jnp.exp(x - top) for x in lses]
        total = functools.reduce(jnp.add, ws)
        packed = pack_rows(top + jnp.log(total), heads)
        stacked = jnp.concatenate([w / total for w in ws], axis=0)
        wt = jnp.transpose(stacked)
        for d in range(group):
            out_ref[g + d, span : span + LSE_ROWS, :] = packed
            for h in range(heads):
                rows = slice(h * lat_local, (h + 1) * lat_local)
                acc = jnp.zeros((lat_local, HEAD_DIM), F32)
                for i, r in enumerate(parts):
                    w = wt[d * lat_local : (d + 1) * lat_local, i * heads + h : i * heads + h + 1]
                    acc = acc + w * r[g + d, rows, :].astype(F32)
                out_ref[g + d, rows, :] = acc.astype(BF16)


def combine_kernel(core_ref, r_ref, w_ref, mlp_ref, own_ref, other_ref, mlp_out, terms_ref, spot_ref, w_vmem, sems, *, lat_local):
    copies = [
        pltpu.make_async_copy(w_ref, w_vmem, sems.at[0]),
        pltpu.make_async_copy(mlp_ref, mlp_out, sems.at[1]),
    ]
    for copy in copies:
        copy.start()
    devices, tall, _ = r_ref.shape
    span = tall - LSE_ROWS
    heads = span // lat_local
    lses = [unpack_rows(r_ref[d, span : span + LSE_ROWS, :], heads) for d in range(devices)]
    top = functools.reduce(jnp.maximum, lses)
    ws = [jnp.exp(x - top) for x in lses]
    total = functools.reduce(jnp.add, ws)
    stacked = jnp.concatenate([w / total for w in ws], axis=0)
    spot_ref[...] = jnp.transpose(stacked)
    wt = spot_ref[pl.ds(pl.multiple_of(core_ref[1], lat_local), lat_local), :]
    parts = []
    for h in range(heads):
        acc = jnp.zeros((lat_local, HEAD_DIM), F32)
        for d in range(devices):
            w = wt[:, d * heads + h : d * heads + h + 1]
            acc = acc + w * r_ref[d, h * lat_local : (h + 1) * lat_local, :].astype(F32)
        parts.append(acc.astype(BF16))
    copies[0].wait()
    terms = jnp.zeros((lat_local, w_vmem.shape[1]), F32)
    for h in range(span // lat_local):
        terms = terms + jnp.dot(
            parts[h],
            w_vmem[h * HEAD_DIM : (h + 1) * HEAD_DIM, :],
            preferred_element_type=F32,
        )
    half = lat_local // 2
    terms_ref[...] = terms.reshape(2, half, w_vmem.shape[1])
    own_ref[...] = terms_ref[core_ref[0]]
    other_ref[...] = terms_ref[1 - core_ref[0]].astype(BF16)
    copies[1].wait()


def spread_kernel(l_ref, w_ref, out_ref, l_vmem, w_vmem, sems):
    copies = [
        pltpu.make_async_copy(w_ref, w_vmem, sems.at[0]),
        pltpu.make_async_copy(l_ref, l_vmem, sems.at[1]),
    ]
    for copy in copies:
        copy.start()
    for copy in copies:
        copy.wait()
    q = jnp.dot(l_vmem[...], w_vmem[...], preferred_element_type=F32).astype(BF16)
    out_ref[...] = jnp.broadcast_to(q[None], out_ref.shape)


def latent_kernel(own_ref, recv_ref, w_ref, out_ref):
    normed = rms_norm(own_ref[...] + recv_ref[...].astype(F32))
    hidden = jax.nn.gelu(jnp.dot(normed.astype(BF16), w_ref[...], preferred_element_type=F32))
    rows = (normed + hidden).astype(BF16)
    out_ref[...] = jnp.broadcast_to(rows[None], out_ref.shape)


def write_kv(row_refs, w_ref, out_ref, first):
    at = 0
    wide = w_ref.shape[1]
    for r in row_refs:
        n = r.shape[0]
        out_ref[at : at + n, first : first + wide] = jnp.dot(
            r[...], w_ref[...], preferred_element_type=F32
        ).astype(BF16)
        at += n


def kv_kernel(*refs):
    *row_refs, k_ref, v_ref, out_ref = refs
    write_kv(row_refs, k_ref, out_ref, 0)
    write_kv(row_refs, v_ref, out_ref, k_ref.shape[1])


def head_columns(columns, h):
    return (
        slice(h * HEAD_DIM, (h + 1) * HEAD_DIM),
        slice(columns + h * HEAD_DIM, columns + (h + 1) * HEAD_DIM),
    )


def near_kernel(q_ref, kv_ref, sums_ref, tops_ref, totals_ref, s_ref):
    columns = q_ref.shape[1]
    shape = (q_ref.shape[0], HEAD_DIM)

    def score(h):
        kc, _ = head_columns(columns, h)
        s_ref[h % 2] = nt_dot(q_ref[:, kc], kv_ref[:, kc])

    def use(h):
        kc, vc = head_columns(columns, h)
        s = s_ref[h % 2]
        m = jnp.max(s, axis=1, keepdims=True)
        p = jnp.exp2((s - m) * (SCALE * LOG2E))
        sums_ref[:, kc] = jnp.dot(p.astype(BF16), kv_ref[:, vc], preferred_element_type=F32)
        tops_ref[:, kc] = jnp.broadcast_to(m, shape)
        totals_ref[:, kc] = jnp.broadcast_to(jnp.sum(p, axis=1, keepdims=True), shape)

    pipelined(columns // HEAD_DIM, score, use)


def attend(q_ref, carried_refs, kv_refs, s_ref, put):
    sums_ref, tops_ref, totals_ref = carried_refs
    columns = q_ref.shape[1]
    spots = []
    at = 0
    for kv in kv_refs:
        spots.append(slice(at, at + kv.shape[0]))
        at += kv.shape[0]

    def score(h):
        kc, _ = head_columns(columns, h)
        for spot, kv in zip(spots, kv_refs):
            s_ref[h % 2, :, spot] = nt_dot(q_ref[:, kc], kv[:, kc])

    def use(h):
        kc, vc = head_columns(columns, h)
        s = s_ref[h % 2]
        before = tops_ref[:, kc]
        m = jnp.maximum(before, jnp.max(s, axis=1, keepdims=True))
        keep = jnp.exp2((before - m) * (SCALE * LOG2E))
        p = jnp.exp2((s - m[:, :1]) * (SCALE * LOG2E))
        total = totals_ref[:, kc] * keep + jnp.sum(p, axis=1, keepdims=True)
        o = sums_ref[:, kc] * keep
        pb = p.astype(BF16)
        for spot, kv in zip(spots, kv_refs):
            o = o + jnp.dot(pb[:, spot], kv[:, vc], preferred_element_type=F32)
        put(kc, o, m, total)

    pipelined(columns // HEAD_DIM, score, use)


def middle_kernel(base_ref, q_ref, *refs):
    carried, (*kv_refs, sums_out, tops_out, totals_out, s_ref) = refs[:3], refs[3:]

    def put(kc, o, m, total):
        sums_out[:, kc] = o
        tops_out[:, kc] = m
        totals_out[:, kc] = total

    attend(q_ref, carried, kv_refs, s_ref, put)


def projected(q_ref, carried, kv_refs, w_ref, s_ref, o_ref):
    def put(kc, o, m, total):
        o_ref[:, kc] = (o / total).astype(BF16)

    attend(q_ref, carried, kv_refs, s_ref, put)
    return jnp.dot(o_ref[...], w_ref[...], preferred_element_type=F32)


def away_kernel(base_ref, q_ref, *refs):
    carried, (*kv_refs, w_ref, out_ref, s_ref, o_ref) = refs[:3], refs[3:]
    out_ref[...] = projected(q_ref, carried, kv_refs, w_ref, s_ref, o_ref).astype(BF16)


def home_kernel(base_ref, q_ref, *refs):
    carried, (*kv_refs, w_ref, recv_ref, out_ref, s_ref, o_ref) = refs[:3], refs[3:]
    terms = projected(q_ref, carried, kv_refs, w_ref, s_ref, o_ref)
    out_ref[...] = rms_norm(terms + recv_ref[...].astype(F32)).astype(BF16)


def full_spec(array):
    return pl.BlockSpec(array.shape, lambda *_: (0,) * array.ndim)


def params(limit=56 << 20):
    return pltpu.CompilerParams(vmem_limit_bytes=limit)


def cross(valid, q, k, v, lat_local, first, heads, before=None):
    lat, columns = q.shape
    tall = (first + heads) * lat_local + LSE_ROWS
    block = min(ROW_BLOCK, lat)
    extra = () if before is None else (before,)
    return pl.pallas_call(
        functools.partial(cross_kernel, lat_local=lat_local, first=first, heads=heads),
        out_shape=jax.ShapeDtypeStruct((lat // lat_local, tall, HEAD_DIM), BF16),
        grid_spec=pltpu.PrefetchScalarGridSpec(
            num_scalar_prefetch=1,
            grid=(lat // block,),
            in_specs=[
                pl.BlockSpec((block, columns), lambda i, c: (i, 0)),
                full_spec(k),
                full_spec(v),
                *[pl.BlockSpec((block // lat_local,) + x.shape[1:], lambda i, c: (i, 0, 0)) for x in extra],
            ],
            out_specs=pl.BlockSpec((block // lat_local, tall, HEAD_DIM), lambda i, c: (i, 0, 0)),
            scratch_shapes=[pltpu.VMEM((2, block, k.shape[0]), F32)],
        ),
        compiler_params=params(32 << 20),
        cost_estimate=pl.CostEstimate(
            flops=4 * lat * k.shape[0] * heads * HEAD_DIM,
            bytes_accessed=4 << 20,
            transcendentals=lat * k.shape[0] * heads,
        ),
        name="cross",
    )(valid, q, k, v, *extra)


def in_hbm(*arrays):
    return [pltpu.with_memory_space_constraint(x, pltpu.HBM) for x in arrays]


def load(arrays):
    return pl.pallas_call(
        load_kernel,
        out_shape=[jax.ShapeDtypeStruct(x.shape, x.dtype) for x in arrays],
        in_specs=[pl.BlockSpec(memory_space=pltpu.HBM)] * len(arrays),
        out_specs=[pl.BlockSpec(memory_space=pltpu.VMEM)] * len(arrays),
        scratch_shapes=[pltpu.SemaphoreType.DMA((len(arrays),))],
        compiler_params=params(8 << 20),
        name="load",
    )(*in_hbm(*arrays))


def join(parts, lat_local):
    vmem = pl.BlockSpec(memory_space=pltpu.VMEM)
    return pl.pallas_call(
        functools.partial(join_kernel, lat_local=lat_local),
        out_shape=jax.ShapeDtypeStruct(parts[0].shape, BF16),
        in_specs=[vmem] * len(parts),
        out_specs=vmem,
        compiler_params=params(24 << 20),
        name="join",
    )(*parts)


def combine(core, gathered, w_out, w_mlp, lat_local):
    width = w_out.shape[1]
    half = lat_local // 2
    vmem = pl.BlockSpec(memory_space=pltpu.VMEM)
    hbm = pl.BlockSpec(memory_space=pltpu.HBM)
    return pl.pallas_call(
        functools.partial(combine_kernel, lat_local=lat_local),
        out_shape=(
            jax.ShapeDtypeStruct((half, width), F32),
            jax.ShapeDtypeStruct((half, width), BF16),
            jax.ShapeDtypeStruct(w_mlp.shape, BF16),
        ),
        in_specs=[pl.BlockSpec(memory_space=pltpu.SMEM), vmem, hbm, hbm],
        out_specs=(vmem, vmem, vmem),
        scratch_shapes=[
            pltpu.VMEM((2, half, width), F32),
            pltpu.VMEM((HEAD_DIM, gathered.shape[0] * (w_out.shape[0] // HEAD_DIM)), F32),
            pltpu.VMEM(w_out.shape, BF16),
            pltpu.SemaphoreType.DMA((2,)),
        ],
        compiler_params=params(24 << 20),
        name="combine",
    )(core, gathered, *in_hbm(w_out, w_mlp))


def spread(latents, w_query, devices):
    hbm = pl.BlockSpec(memory_space=pltpu.HBM)
    return pl.pallas_call(
        spread_kernel,
        out_shape=jax.ShapeDtypeStruct((devices, latents.shape[0], w_query.shape[1]), BF16),
        in_specs=[hbm, hbm],
        out_specs=pl.BlockSpec(memory_space=pltpu.VMEM),
        scratch_shapes=[
            pltpu.VMEM(latents.shape, BF16),
            pltpu.VMEM(w_query.shape, BF16),
            pltpu.SemaphoreType.DMA((2,)),
        ],
        compiler_params=params(60 << 20),
        name="spread",
    )(*in_hbm(latents, w_query))


def latent_rows(own, recv, w_mlp, devices):
    vmem = pl.BlockSpec(memory_space=pltpu.VMEM)
    return pl.pallas_call(
        latent_kernel,
        out_shape=jax.ShapeDtypeStruct((devices,) + own.shape, BF16),
        in_specs=[vmem] * 3,
        out_specs=vmem,
        compiler_params=params(24 << 20),
        name="latent",
    )(own, recv, w_mlp)


def latent_kv(rows, w_lkey, w_lvalue):
    vmem = pl.BlockSpec(memory_space=pltpu.VMEM)
    total = sum(r.shape[0] for r in rows)
    wide = w_lkey.shape[1] * 2
    return pl.pallas_call(
        kv_kernel,
        out_shape=jax.ShapeDtypeStruct((total, wide), BF16),
        in_specs=[vmem] * (len(rows) + 2),
        out_specs=vmem,
        compiler_params=params(24 << 20),
        cost_estimate=pl.CostEstimate(
            flops=2 * total * wide * w_lkey.shape[0], bytes_accessed=4 << 20, transcendentals=0
        ),
        name="latent_kv",
    )(*rows, w_lkey, w_lvalue)


def near_decode(q, kv):
    rows, columns = q.shape
    block = ROW_BLOCK
    return pl.pallas_call(
        near_kernel,
        out_shape=(
            jax.ShapeDtypeStruct((rows, columns), F32),
        )
        * 3,
        grid=(rows // block,),
        in_specs=[pl.BlockSpec((block, columns), lambda i: (i, 0)), full_spec(kv)],
        out_specs=(pl.BlockSpec((block, columns), lambda i: (i, 0)),) * 3,
        scratch_shapes=[pltpu.VMEM((2, block, kv.shape[0]), F32)],
        compiler_params=params(24 << 20),
        cost_estimate=pl.CostEstimate(
            flops=4 * rows * columns * kv.shape[0], bytes_accessed=4 << 20, transcendentals=4 * rows * kv.shape[0]
        ),
        name="near_decode",
    )(q, kv)


def decode(kernel, base, q, carried, kvs, w_pout=None, recv=None):
    rows, columns = q.shape[0] // 2, q.shape[1]
    block = min(ROW_BLOCK, rows)
    keys = sum(kv.shape[0] for kv in kvs)
    blocks = rows // block

    def at_base(x):
        if x.shape[0] == rows:
            return pl.BlockSpec((block, x.shape[1]), lambda i, b: (i, 0))
        return pl.BlockSpec((block, x.shape[1]), lambda i, b: (b[0] * blocks + i, 0))

    scratch = [pltpu.VMEM((2, block, keys), F32)]
    if w_pout is None:
        out_shape = (jax.ShapeDtypeStruct((rows, columns), F32),) * 3
        out_specs = (pl.BlockSpec((block, columns), lambda i, b: (i, 0)),) * 3
        extra, extra_specs = (), []
    else:
        width = w_pout.shape[1]
        out_shape = jax.ShapeDtypeStruct((rows, width), BF16)
        out_specs = pl.BlockSpec((block, width), lambda i, b: (i, 0))
        scratch.append(pltpu.VMEM((block, columns), BF16))
        extra = (w_pout,) if recv is None else (w_pout, recv)
        extra_specs = [full_spec(w_pout)] + ([] if recv is None else [at_base(recv)])
    return pl.pallas_call(
        kernel,
        out_shape=out_shape,
        grid_spec=pltpu.PrefetchScalarGridSpec(
            num_scalar_prefetch=1,
            grid=(blocks,),
            in_specs=[*[at_base(x) for x in (q, *carried)], *[full_spec(x) for x in kvs], *extra_specs],
            out_specs=out_specs,
            scratch_shapes=scratch,
        ),
        compiler_params=params(30 << 20),
        cost_estimate=pl.CostEstimate(
            flops=4 * rows * columns * keys, bytes_accessed=8 << 20, transcendentals=4 * rows * keys
        ),
        name="decode",
    )(base, q, *carried, *kvs, *extra)


def project(a, w):
    return jnp.dot(a, w, preferred_element_type=F32).astype(BF16)


def per_device(
    inputs,
    valid_blocks,
    latents,
    w_query,
    w_key,
    w_value,
    w_out,
    w_mlp,
    w_lkey,
    w_lvalue,
    w_pquery,
    w_pout,
):
    lat_local = latents.shape[0]
    columns = w_key.shape[1]
    width = inputs.shape[1]
    core = lax.axis_index("head").astype(jnp.int32).reshape(1)
    swap = [(0, 1), (1, 0)]

    plane, long = plane_groups()

    def within_plane(x):
        return lax.all_to_all(x, AXES, 0, 0, axis_index_groups=plane)

    def along(x, shift):
        return lax.ppermute(x, AXES, long[shift % SIDE])

    queries = within_plane(spread(latents, w_query, SIDE * SIDE)).reshape(-1, columns)
    keys = project(inputs, w_key)
    values = project(inputs, w_value)
    queries, keys, values = lax.optimization_barrier((queries, keys, values))
    away = [along(queries, s) for s in ORDER]
    keys, values = load((keys, values))
    heads = columns // HEAD_DIM
    half = cross(valid_blocks, queries, keys, values, lat_local, 0, heads // 2)
    part, partials = half, []
    for s, there in zip(ORDER, away):
        part, there = lax.optimization_barrier((part, there))
        part = cross(valid_blocks, there, keys, values, lat_local, 0, heads)
        partials.append(along(part, -s))
    part, half = lax.optimization_barrier((part, half))
    stay = cross(valid_blocks, queries, keys, values, lat_local, heads // 2, heads // 2, half)
    *early, late = partials
    stay, late = lax.optimization_barrier((join([stay, *early], lat_local), late))
    partials = [stay, late]
    gathered = within_plane(join(partials, lat_local))
    own, other, w_mlp = combine(jnp.concatenate([core, lane_offset(lat_local)]), gathered, w_out, w_mlp, lat_local)
    recv = lax.ppermute(other, "head", swap)
    rows = latent_rows(own, recv, w_mlp, SIDE * SIDE)
    rows, inputs = lax.optimization_barrier((rows, inputs))
    pos_queries = project(inputs, w_pquery)
    near, pos_queries = lax.optimization_barrier((within_plane(rows), pos_queries))
    near = near.reshape(-1, width)
    quick = []
    for s in (1, 3):
        quick.append(along(near, s))
    near_swapped = lax.ppermute(near, "head", swap)
    near, w_lkey, w_lvalue, w_pout = lax.optimization_barrier((near, w_lkey, w_lvalue, w_pout))
    w_lkey, w_lvalue, w_pout = load((w_lkey, w_lvalue, w_pout))
    kv = latent_kv([near, near_swapped], w_lkey, w_lvalue)
    near, kv = lax.optimization_barrier((near, kv))
    slow = along(near, 2)
    carried = near_decode(pos_queries, kv)
    carried, quick = lax.optimization_barrier((carried, quick))
    quick_swapped = [lax.ppermute(x, "head", swap) for x in quick]
    quick_kv = latent_kv(quick, w_lkey, w_lvalue)
    swapped_kv = latent_kv(quick_swapped, w_lkey, w_lvalue)
    further = decode(middle_kernel, 1 - core, pos_queries, carried, [quick_kv, swapped_kv])
    slow, further = lax.optimization_barrier((slow, further))
    slow_swapped = lax.ppermute(slow, "head", swap)
    slow_kv = latent_kv([slow], w_lkey, w_lvalue)
    slow_swapped_kv = latent_kv([slow_swapped], w_lkey, w_lvalue)
    slow_kvs = [slow_kv, slow_swapped_kv]
    terms = decode(away_kernel, 1 - core, pos_queries, further, slow_kvs, w_pout)
    arrived = lax.ppermute(terms, "head", swap)
    return decode(home_kernel, core, pos_queries, carried, [quick_kv, swapped_kv, *slow_kvs], w_pout, arrived)


def solution(mesh):
    placed = (
        P("pos", None),
        P("pos"),
        P("pos", None),
        P(None, "head"),
        P(None, "head"),
        P(None, "head"),
        P("head", None),
        P(),
        P(None, "head"),
        P(None, "head"),
        P(None, "head"),
        P("head", None),
    )

    return jax.shard_map(
        per_device,
        mesh=mesh,
        in_specs=placed,
        out_specs=P(("pos", "head"), None),
        check_vma=False,
    )
```

```python
import functools

import jax
import jax.numpy as jnp
from jax import lax
from jax.experimental import pallas as pl
from jax.experimental.pallas import tpu as pltpu
from jax.sharding import PartitionSpec as P


HEAD_DIM = 128
BLK = 128
SCALE = HEAD_DIM ** (-0.5)
LOG2E = 1.4426950408889634
MASKED = -1e30
EPS = 1e-05
F32 = jnp.float32
BF16 = jnp.bfloat16
ROW_BLOCK = 256
LSE_ROWS = 16


AXES = ("pos", "head")
SIDE = 4
ORDER = (1, 2, 3)
FAR_ORDER = (2, 1, 3)


def plane_groups():
    def device(z, y, x, core):
        return ((z * SIDE + y) * SIDE + x) * 2 + core

    r = range(SIDE)
    plane = [[device(z, y, x, 0) for y in r for x in r] for z in r]
    plane += [[device(z, y, x, 1) for z in r for x in r] for y in r]
    long = {}
    for s in range(1, SIDE):
        long[s] = [
            pair
            for z in r
            for y in r
            for x in r
            for pair in (
                (device(z, y, x, 0), device((z + s) % SIDE, y, x, 0)),
                (device(z, y, x, 1), device(z, (y + s) % SIDE, x, 1)),
            )
        ]
    return plane, long


def lane_offset(lat_local):
    x = lax.axis_index("pos") % SIDE
    return (x % (HEAD_DIM // lat_local) * lat_local).astype(jnp.int32).reshape(1)


def rms_norm(values):
    return values * lax.rsqrt(jnp.mean(values * values, axis=-1, keepdims=True) + EPS)


def nt_dot(a, b):
    return lax.dot_general(a, b, (((1,), (1,)), ((), ())), preferred_element_type=F32)


def bf16_pieces(x):
    hi = x.astype(BF16).astype(F32)
    mid = (x - hi).astype(BF16).astype(F32)
    low = (x - hi - mid).astype(BF16).astype(F32)
    return hi, mid, low


def pack_rows(lse, heads):
    rows = jnp.concatenate([p[:heads] for p in bf16_pieces(lse)], axis=0)
    pad = jnp.zeros((LSE_ROWS - rows.shape[0], rows.shape[1]), F32)
    return jnp.concatenate([rows, pad], axis=0).astype(BF16)


def unpack_rows(packed, heads):
    x = packed.astype(F32)
    return x[:heads] + x[heads : 2 * heads] + x[2 * heads : 3 * heads]


def pipelined(count, score, use):
    score(0)
    for i in range(count):
        if i + 1 < count:
            score(i + 1)
        use(i)


def cross_kernel(valid_ref, q_ref, k_ref, v_ref, *refs, lat_local, first, heads):
    *before, out_ref, s_ref = refs
    rows = q_ref.shape[0]
    owners = rows // lat_local
    all_heads = q_ref.shape[1] // HEAD_DIM
    done = first * lat_local
    span = done + heads * lat_local
    keys = k_ref.shape[0]
    valid = sum(valid_ref[i] for i in range(keys // BLK)) * BLK
    live = lax.broadcasted_iota(jnp.int32, (1, keys), 1) < valid
    bias = jnp.where(live, 0.0, MASKED)
    lane = lax.broadcasted_iota(jnp.int32, (rows, HEAD_DIM), 1)
    if before:
        out_ref[:, :done, :] = before[0][:, :done, :]
    tops = jnp.zeros((rows, HEAD_DIM), F32)
    totals = jnp.ones((rows, HEAD_DIM), F32)

    def columns(i):
        return slice((first + i) * HEAD_DIM, (first + i + 1) * HEAD_DIM)

    def score(i):
        s_ref[i % 2] = nt_dot(q_ref[:, columns(i)], k_ref[:, columns(i)]) + bias

    def use(i):
        nonlocal tops, totals
        s = s_ref[i % 2]
        m = jnp.max(s, axis=1, keepdims=True)
        p = jnp.exp2((s - m) * (SCALE * LOG2E))
        total = jnp.sum(p, axis=1, keepdims=True)
        o = jnp.dot(p.astype(BF16), v_ref[:, columns(i)], preferred_element_type=F32)
        o = (o / total).astype(BF16)
        top = (first + i) * lat_local
        out_ref[:, top : top + lat_local, :] = o.reshape(owners, lat_local, HEAD_DIM)
        mine = lane % all_heads == first + i
        tops = jnp.where(mine, m, tops)
        totals = jnp.where(mine, total, totals)

    pipelined(heads, score, use)
    hi, mid, low = bf16_pieces(tops * SCALE + jnp.log(totals))
    place = lane // all_heads
    packed = jnp.where(place == 0, hi, jnp.where(place == 1, mid, jnp.where(place == 2, low, 0.0)))
    eye = lax.broadcasted_iota(jnp.int32, (LSE_ROWS, HEAD_DIM), 0)
    eye = (eye == lax.broadcasted_iota(jnp.int32, (LSE_ROWS, HEAD_DIM), 1)).astype(BF16)
    turned = nt_dot(eye, packed.astype(BF16)).astype(BF16)
    for d in range(owners):
        at = d * lat_local // HEAD_DIM * HEAD_DIM
        rows_d = turned[:, at : at + HEAD_DIM]
        if before:
            rows_d = rows_d + before[0][d, done : done + LSE_ROWS, :]
        out_ref[d, span : span + LSE_ROWS, :] = rows_d


def load_kernel(*refs):
    n = len(refs) // 2
    *pairs, sems = refs
    copies = [pltpu.make_async_copy(pairs[i], pairs[n + i], sems.at[i]) for i in range(n)]
    for copy in copies:
        copy.start()
    for copy in copies:
        copy.wait()


def join_kernel(*refs, lat_local):
    *parts, out_ref = refs
    owners, tall, _ = out_ref.shape
    span = tall - LSE_ROWS
    heads = span // lat_local
    group = HEAD_DIM // lat_local
    whole = [r for r in parts if r.shape[0] == owners]
    split = [r for r in parts if r.shape[0] != owners]
    for g in range(0, owners, group):
        parts = [(r, g) for r in whole]
        if split:
            parts.append((split[g // split[0].shape[0]], g % split[0].shape[0]))
        lses = [unpack_rows(r[at, span : span + LSE_ROWS, :], heads) for r, at in parts]
        top = functools.reduce(jnp.maximum, lses)
        ws = [jnp.exp(x - top) for x in lses]
        total = functools.reduce(jnp.add, ws)
        packed = pack_rows(top + jnp.log(total), heads)
        stacked = jnp.concatenate([w / total for w in ws], axis=0)
        wt = jnp.transpose(stacked)
        for d in range(group):
            out_ref[g + d, span : span + LSE_ROWS, :] = packed
            for h in range(heads):
                rows = slice(h * lat_local, (h + 1) * lat_local)
                acc = jnp.zeros((lat_local, HEAD_DIM), F32)
                for i, (r, at) in enumerate(parts):
                    w = wt[d * lat_local : (d + 1) * lat_local, i * heads + h : i * heads + h + 1]
                    acc = acc + w * r[at + d, rows, :].astype(F32)
                out_ref[g + d, rows, :] = acc.astype(BF16)


def combine_kernel(core_ref, r_ref, w_ref, mlp_ref, own_ref, other_ref, mlp_out, terms_ref, spot_ref, w_vmem, sems, *, lat_local):
    copies = [
        pltpu.make_async_copy(w_ref, w_vmem, sems.at[0]),
        pltpu.make_async_copy(mlp_ref, mlp_out, sems.at[1]),
    ]
    for copy in copies:
        copy.start()
    devices, tall, _ = r_ref.shape
    span = tall - LSE_ROWS
    heads = span // lat_local
    lses = [unpack_rows(r_ref[d, span : span + LSE_ROWS, :], heads) for d in range(devices)]
    top = functools.reduce(jnp.maximum, lses)
    ws = [jnp.exp(x - top) for x in lses]
    total = functools.reduce(jnp.add, ws)
    stacked = jnp.concatenate([w / total for w in ws], axis=0)
    spot_ref[...] = jnp.transpose(stacked)
    wt = spot_ref[pl.ds(pl.multiple_of(core_ref[1], lat_local), lat_local), :]
    parts = []
    for h in range(heads):
        acc = jnp.zeros((lat_local, HEAD_DIM), F32)
        for d in range(devices):
            w = wt[:, d * heads + h : d * heads + h + 1]
            acc = acc + w * r_ref[d, h * lat_local : (h + 1) * lat_local, :].astype(F32)
        parts.append(acc.astype(BF16))
    copies[0].wait()
    terms = jnp.zeros((lat_local, w_vmem.shape[1]), F32)
    for h in range(span // lat_local):
        terms = terms + jnp.dot(
            parts[h],
            w_vmem[h * HEAD_DIM : (h + 1) * HEAD_DIM, :],
            preferred_element_type=F32,
        )
    half = lat_local // 2
    terms_ref[...] = terms.reshape(2, half, w_vmem.shape[1])
    own_ref[...] = terms_ref[core_ref[0]]
    other_ref[...] = terms_ref[1 - core_ref[0]].astype(BF16)
    copies[1].wait()


def spread_kernel(l_ref, w_ref, out_ref, l_vmem, w_vmem, sems):
    copies = [
        pltpu.make_async_copy(w_ref, w_vmem, sems.at[0]),
        pltpu.make_async_copy(l_ref, l_vmem, sems.at[1]),
    ]
    for copy in copies:
        copy.start()
    for copy in copies:
        copy.wait()
    q = jnp.dot(l_vmem[...], w_vmem[...], preferred_element_type=F32).astype(BF16)
    out_ref[...] = jnp.broadcast_to(q[None], out_ref.shape)


def latent_kernel(own_ref, recv_ref, w_ref, out_ref):
    normed = rms_norm(own_ref[...] + recv_ref[...].astype(F32))
    hidden = jax.nn.gelu(jnp.dot(normed.astype(BF16), w_ref[...], preferred_element_type=F32))
    rows = (normed + hidden).astype(BF16)
    out_ref[...] = jnp.broadcast_to(rows[None], out_ref.shape)


def write_kv(row_refs, w_ref, out_ref, first):
    at = 0
    wide = w_ref.shape[1]
    for r in row_refs:
        n = r.shape[0]
        out_ref[at : at + n, first : first + wide] = jnp.dot(
            r[...], w_ref[...], preferred_element_type=F32
        ).astype(BF16)
        at += n


def kv_kernel(*refs):
    *row_refs, k_ref, v_ref, out_ref = refs
    write_kv(row_refs, k_ref, out_ref, 0)
    write_kv(row_refs, v_ref, out_ref, k_ref.shape[1])


def near_kv_kernel(near_ref, swapped_ref, k_ref, v_ref, p_ref, out_ref, k_out, v_out, p_out, sems):
    pairs = ((k_ref, k_out), (v_ref, v_out), (p_ref, p_out))
    copies = [pltpu.make_async_copy(a, b, sems.at[i]) for i, (a, b) in enumerate(pairs)]
    for copy in copies:
        copy.start()
    rows = (near_ref, swapped_ref)
    copies[0].wait()
    write_kv(rows, k_out, out_ref, 0)
    copies[1].wait()
    write_kv(rows, v_out, out_ref, k_out.shape[1])
    copies[2].wait()


def head_columns(columns, h):
    return (
        slice(h * HEAD_DIM, (h + 1) * HEAD_DIM),
        slice(columns + h * HEAD_DIM, columns + (h + 1) * HEAD_DIM),
    )


def near_kernel(q_ref, kv_ref, sums_ref, tops_ref, totals_ref, s_ref):
    columns = q_ref.shape[1]
    shape = (q_ref.shape[0], HEAD_DIM)

    def score(h):
        kc, _ = head_columns(columns, h)
        s_ref[h % 2] = nt_dot(q_ref[:, kc], kv_ref[:, kc])

    def use(h):
        kc, vc = head_columns(columns, h)
        s = s_ref[h % 2]
        m = jnp.max(s, axis=1, keepdims=True)
        p = jnp.exp2((s - m) * (SCALE * LOG2E))
        sums_ref[:, kc] = jnp.dot(p.astype(BF16), kv_ref[:, vc], preferred_element_type=F32)
        tops_ref[:, kc] = jnp.broadcast_to(m, shape)
        totals_ref[:, kc] = jnp.broadcast_to(jnp.sum(p, axis=1, keepdims=True), shape)

    pipelined(columns // HEAD_DIM, score, use)


def attend(q_ref, carried_refs, kv_refs, w_ref, s_ref, o_ref):
    sums_ref, tops_ref, totals_ref = carried_refs
    columns = q_ref.shape[1]
    spots = []
    at = 0
    for kv in kv_refs:
        spots.append(slice(at, at + kv.shape[0]))
        at += kv.shape[0]

    def score(h):
        kc, _ = head_columns(columns, h)
        for spot, kv in zip(spots, kv_refs):
            s_ref[h % 2, :, spot] = nt_dot(q_ref[:, kc], kv[:, kc])

    def use(h):
        kc, vc = head_columns(columns, h)
        s = s_ref[h % 2]
        before = tops_ref[:, kc]
        m = jnp.maximum(before, jnp.max(s, axis=1, keepdims=True))
        keep = jnp.exp2((before - m) * (SCALE * LOG2E))
        p = jnp.exp2((s - m[:, :1]) * (SCALE * LOG2E))
        total = totals_ref[:, kc] * keep + jnp.sum(p, axis=1, keepdims=True)
        o = sums_ref[:, kc] * keep
        pb = p.astype(BF16)
        for spot, kv in zip(spots, kv_refs):
            o = o + jnp.dot(pb[:, spot], kv[:, vc], preferred_element_type=F32)
        o_ref[:, kc] = (o / total).astype(BF16)

    pipelined(columns // HEAD_DIM, score, use)
    return jnp.dot(o_ref[...], w_ref[...], preferred_element_type=F32)


def decode_kernel(base_ref, q_ref, *refs):
    carried, (*kv_refs, w_ref, out_ref, s_ref, o_ref) = refs[:3], refs[3:]
    out_ref[...] = attend(q_ref, carried, kv_refs, w_ref, s_ref, o_ref).astype(out_ref.dtype)


def last_kernel(base_ref, q_ref, *refs):
    carried, (*kv_refs, w_ref, first_ref, recv_ref, out_ref, s_ref, o_ref) = refs[:3], refs[3:]
    n = first_ref.shape[0]
    out_ref[:n] = rms_norm(first_ref[...] + recv_ref[:n].astype(F32)).astype(out_ref.dtype)
    terms = attend(q_ref, carried, kv_refs, w_ref, s_ref, o_ref)
    out_ref[n:] = rms_norm(terms + recv_ref[n:].astype(F32)).astype(out_ref.dtype)


def full_spec(array):
    return pl.BlockSpec(array.shape, lambda *_: (0,) * array.ndim)


def params(limit=56 << 20):
    return pltpu.CompilerParams(vmem_limit_bytes=limit)


def cross(valid, q, k, v, lat_local, first, heads, before=None, block_at=0, blocks=None):
    columns = q.shape[1]
    tall = (first + heads) * lat_local + LSE_ROWS
    block = min(ROW_BLOCK, q.shape[0])
    blocks = q.shape[0] // block if blocks is None else blocks
    lat = blocks * block
    extra = () if before is None else (before,)
    return pl.pallas_call(
        functools.partial(cross_kernel, lat_local=lat_local, first=first, heads=heads),
        out_shape=jax.ShapeDtypeStruct((lat // lat_local, tall, HEAD_DIM), BF16),
        grid_spec=pltpu.PrefetchScalarGridSpec(
            num_scalar_prefetch=1,
            grid=(lat // block,),
            in_specs=[
                pl.BlockSpec((block, columns), lambda i, c: (block_at + i, 0)),
                full_spec(k),
                full_spec(v),
                *[pl.BlockSpec((block // lat_local,) + x.shape[1:], lambda i, c: (i, 0, 0)) for x in extra],
            ],
            out_specs=pl.BlockSpec((block // lat_local, tall, HEAD_DIM), lambda i, c: (i, 0, 0)),
            scratch_shapes=[pltpu.VMEM((2, block, k.shape[0]), F32)],
        ),
        compiler_params=params(32 << 20),
        cost_estimate=pl.CostEstimate(
            flops=4 * lat * k.shape[0] * heads * HEAD_DIM,
            bytes_accessed=4 << 20,
            transcendentals=lat * k.shape[0] * heads,
        ),
        name="cross",
    )(valid, q, k, v, *extra)


def in_hbm(*arrays):
    return [pltpu.with_memory_space_constraint(x, pltpu.HBM) for x in arrays]


def load(arrays):
    return pl.pallas_call(
        load_kernel,
        out_shape=[jax.ShapeDtypeStruct(x.shape, x.dtype) for x in arrays],
        in_specs=[pl.BlockSpec(memory_space=pltpu.HBM)] * len(arrays),
        out_specs=[pl.BlockSpec(memory_space=pltpu.VMEM)] * len(arrays),
        scratch_shapes=[pltpu.SemaphoreType.DMA((len(arrays),))],
        compiler_params=params(8 << 20),
        name="load",
    )(*in_hbm(*arrays))


def join(parts, lat_local):
    vmem = pl.BlockSpec(memory_space=pltpu.VMEM)
    return pl.pallas_call(
        functools.partial(join_kernel, lat_local=lat_local),
        out_shape=jax.ShapeDtypeStruct(parts[0].shape, BF16),
        in_specs=[vmem] * len(parts),
        out_specs=vmem,
        compiler_params=params(24 << 20),
        name="join",
    )(*parts)


def combine(core, gathered, w_out, w_mlp, lat_local):
    width = w_out.shape[1]
    half = lat_local // 2
    vmem = pl.BlockSpec(memory_space=pltpu.VMEM)
    hbm = pl.BlockSpec(memory_space=pltpu.HBM)
    return pl.pallas_call(
        functools.partial(combine_kernel, lat_local=lat_local),
        out_shape=(
            jax.ShapeDtypeStruct((half, width), F32),
            jax.ShapeDtypeStruct((half, width), BF16),
            jax.ShapeDtypeStruct(w_mlp.shape, BF16),
        ),
        in_specs=[pl.BlockSpec(memory_space=pltpu.SMEM), vmem, hbm, hbm],
        out_specs=(vmem, vmem, vmem),
        scratch_shapes=[
            pltpu.VMEM((2, half, width), F32),
            pltpu.VMEM((HEAD_DIM, gathered.shape[0] * (w_out.shape[0] // HEAD_DIM)), F32),
            pltpu.VMEM(w_out.shape, BF16),
            pltpu.SemaphoreType.DMA((2,)),
        ],
        compiler_params=params(24 << 20),
        name="combine",
    )(core, gathered, *in_hbm(w_out, w_mlp))


def spread(latents, w_query, devices):
    hbm = pl.BlockSpec(memory_space=pltpu.HBM)
    return pl.pallas_call(
        spread_kernel,
        out_shape=jax.ShapeDtypeStruct((devices, latents.shape[0], w_query.shape[1]), BF16),
        in_specs=[hbm, hbm],
        out_specs=pl.BlockSpec(memory_space=pltpu.VMEM),
        scratch_shapes=[
            pltpu.VMEM(latents.shape, BF16),
            pltpu.VMEM(w_query.shape, BF16),
            pltpu.SemaphoreType.DMA((2,)),
        ],
        compiler_params=params(60 << 20),
        name="spread",
    )(*in_hbm(latents, w_query))


def latent_rows(own, recv, w_mlp, devices):
    vmem = pl.BlockSpec(memory_space=pltpu.VMEM)
    return pl.pallas_call(
        latent_kernel,
        out_shape=jax.ShapeDtypeStruct((devices,) + own.shape, BF16),
        in_specs=[vmem] * 3,
        out_specs=vmem,
        compiler_params=params(24 << 20),
        name="latent",
    )(own, recv, w_mlp)


def latent_kv(rows, w_lkey, w_lvalue):
    vmem = pl.BlockSpec(memory_space=pltpu.VMEM)
    total = sum(r.shape[0] for r in rows)
    wide = w_lkey.shape[1] * 2
    return pl.pallas_call(
        kv_kernel,
        out_shape=jax.ShapeDtypeStruct((total, wide), BF16),
        in_specs=[vmem] * (len(rows) + 2),
        out_specs=vmem,
        compiler_params=params(24 << 20),
        cost_estimate=pl.CostEstimate(
            flops=2 * total * wide * w_lkey.shape[0], bytes_accessed=4 << 20, transcendentals=0
        ),
        name="latent_kv",
    )(*rows, w_lkey, w_lvalue)


def near_kv(near, swapped, w_lkey, w_lvalue, w_pout):
    vmem = pl.BlockSpec(memory_space=pltpu.VMEM)
    hbm = pl.BlockSpec(memory_space=pltpu.HBM)
    rows = near.shape[0] + swapped.shape[0]
    return pl.pallas_call(
        near_kv_kernel,
        out_shape=[
            jax.ShapeDtypeStruct((rows, 2 * w_lkey.shape[1]), BF16),
            *[jax.ShapeDtypeStruct(w.shape, BF16) for w in (w_lkey, w_lvalue, w_pout)],
        ],
        in_specs=[vmem, vmem, hbm, hbm, hbm],
        out_specs=[vmem] * 4,
        scratch_shapes=[pltpu.SemaphoreType.DMA((3,))],
        compiler_params=params(24 << 20),
        cost_estimate=pl.CostEstimate(
            flops=4 * rows * w_lkey.size // 2, bytes_accessed=4 << 20, transcendentals=0
        ),
        name="near_kv",
    )(near, swapped, *in_hbm(w_lkey, w_lvalue, w_pout))


def near_decode(q, kv):
    rows, columns = q.shape
    block = ROW_BLOCK
    return pl.pallas_call(
        near_kernel,
        out_shape=(
            jax.ShapeDtypeStruct((rows, columns), F32),
        )
        * 3,
        grid=(rows // block,),
        in_specs=[pl.BlockSpec((block, columns), lambda i: (i, 0)), full_spec(kv)],
        out_specs=(pl.BlockSpec((block, columns), lambda i: (i, 0)),) * 3,
        scratch_shapes=[pltpu.VMEM((2, block, kv.shape[0]), F32)],
        compiler_params=params(24 << 20),
        cost_estimate=pl.CostEstimate(
            flops=4 * rows * columns * kv.shape[0], bytes_accessed=4 << 20, transcendentals=4 * rows * kv.shape[0]
        ),
        name="near_decode",
    )(q, kv)


def decode(base, blocks, q, carried, kvs, w_pout, dtype, finish=()):
    columns = q.shape[1]
    width = w_pout.shape[1]
    block = ROW_BLOCK
    rows = blocks * block
    out_rows = finish[1].shape[0] if finish else rows
    out_block = out_rows if finish else block
    keys = sum(kv.shape[0] for kv in kvs)
    return pl.pallas_call(
        last_kernel if finish else decode_kernel,
        out_shape=jax.ShapeDtypeStruct((out_rows, width), dtype),
        grid_spec=pltpu.PrefetchScalarGridSpec(
            num_scalar_prefetch=1,
            grid=(blocks,),
            in_specs=[
                *[pl.BlockSpec((block, x.shape[1]), lambda i, b: (b[0] + i, 0)) for x in (q, *carried)],
                *[full_spec(x) for x in (*kvs, w_pout, *finish)],
            ],
            out_specs=pl.BlockSpec((out_block, width), lambda i, b: (i, 0)),
            scratch_shapes=[pltpu.VMEM((2, block, keys), F32), pltpu.VMEM((block, columns), BF16)],
        ),
        compiler_params=params(36 << 20),
        cost_estimate=pl.CostEstimate(
            flops=4 * rows * columns * keys, bytes_accessed=8 << 20, transcendentals=4 * rows * keys
        ),
        name="decode",
    )(base, q, *carried, *kvs, w_pout, *finish)


def project(a, w):
    return jnp.dot(a, w, preferred_element_type=F32).astype(BF16)


def per_device(
    inputs,
    valid_blocks,
    latents,
    w_query,
    w_key,
    w_value,
    w_out,
    w_mlp,
    w_lkey,
    w_lvalue,
    w_pquery,
    w_pout,
):
    lat_local = latents.shape[0]
    columns = w_key.shape[1]
    width = inputs.shape[1]
    core = lax.axis_index("head").astype(jnp.int32).reshape(1)
    swap = [(0, 1), (1, 0)]

    plane, long = plane_groups()

    def within_plane(x):
        return lax.all_to_all(x, AXES, 0, 0, axis_index_groups=plane)

    def along(x, shift):
        return lax.ppermute(x, AXES, long[shift % SIDE])

    queries = within_plane(spread(latents, w_query, SIDE * SIDE)).reshape(-1, columns)
    keys = project(inputs, w_key)
    values = project(inputs, w_value)
    places = jnp.concatenate([core, lane_offset(lat_local)])
    queries, keys, values, places = lax.optimization_barrier((queries, keys, values, places))
    away = [along(queries, s) for s in ORDER]
    keys, values = load((keys, values))
    heads = columns // HEAD_DIM
    half = cross(valid_blocks, queries, keys, values, lat_local, 0, heads // 2)
    part, partials = half, []
    *soon, final = ORDER
    for s, there in zip(soon, away):
        part, there = lax.optimization_barrier((part, there))
        part = cross(valid_blocks, there, keys, values, lat_local, 0, heads)
        partials.append(along(part, -s))
    there, late = away[-1], []
    for i in range(2):
        part, there = lax.optimization_barrier((part, there))
        part = cross(valid_blocks, there, keys, values, lat_local, 0, heads, None, i, 1)
        late.append(along(part, -final))
    part, half, inputs = lax.optimization_barrier((part, half, inputs))
    stay = cross(valid_blocks, queries, keys, values, lat_local, heads // 2, heads // 2, half)
    pos_queries = project(inputs, w_pquery)
    stay, pos_queries, late = lax.optimization_barrier((join([stay, *partials], lat_local), pos_queries, late))
    partials = [stay, *late]
    gathered = within_plane(join(partials, lat_local))
    own, other, w_mlp = combine(places, gathered, w_out, w_mlp, lat_local)
    recv = lax.ppermute(other, "head", swap)
    rows = latent_rows(own, recv, w_mlp, SIDE * SIDE)
    near = within_plane(rows)
    near = near.reshape(-1, width)
    far = []
    for s in FAR_ORDER:
        far.append(along(near, s))
    near_swapped = lax.ppermute(near, "head", swap)
    kv, w_lkey, w_lvalue, w_pout = near_kv(near, near_swapped, w_lkey, w_lvalue, w_pout)
    carried = near_decode(pos_queries, kv)
    slow, *quick = far
    carried, quick = lax.optimization_barrier((carried, quick))
    quick_swapped = [lax.ppermute(x, "head", swap) for x in quick]
    quick_kv = latent_kv(quick, w_lkey, w_lvalue)
    slow, quick_kv = lax.optimization_barrier((slow, quick_kv))
    slow_swapped = lax.ppermute(slow, "head", swap)
    swapped_kv = latent_kv(quick_swapped, w_lkey, w_lvalue)
    slow_kv = latent_kv([slow, slow_swapped], w_lkey, w_lvalue)
    kvs = [quick_kv, swapped_kv, slow_kv]
    blocks = pos_queries.shape[0] // 2 // ROW_BLOCK
    terms = decode((1 - core) * blocks, blocks, pos_queries, carried, kvs, w_pout, BF16)
    arrived = lax.ppermute(terms, "head", swap)
    first = decode(core * blocks, blocks - 1, pos_queries, carried, kvs, w_pout, F32)
    return decode(core * blocks + blocks - 1, 1, pos_queries, carried, kvs, w_pout, BF16, (first, arrived))


def solution(mesh):
    placed = (
        P("pos", None),
        P("pos"),
        P("pos", None),
        P(None, "head"),
        P(None, "head"),
        P(None, "head"),
        P("head", None),
        P(),
        P(None, "head"),
        P(None, "head"),
        P(None, "head"),
        P("head", None),
    )

    return jax.shard_map(
        per_device,
        mesh=mesh,
        in_specs=placed,
        out_specs=P(("pos", "head"), None),
        check_vma=False,
    )
```

```python
import functools

import jax
import jax.numpy as jnp
from jax import lax
from jax.experimental import pallas as pl
from jax.experimental.pallas import tpu as pltpu
from jax.sharding import PartitionSpec as P


HEAD_DIM = 128
BLK = 128
SCALE = HEAD_DIM ** (-0.5)
LOG2E = 1.4426950408889634
MASKED = -1e30
EPS = 1e-05
F32 = jnp.float32
BF16 = jnp.bfloat16
ROW_BLOCK = 256
LSE_ROWS = 16


AXES = ("pos", "head")
SIDE = 4
ORDER = (1, 2, 3)
FAR_ORDER = (2, 1, 3)


def plane_groups():
    def device(z, y, x, core):
        return ((z * SIDE + y) * SIDE + x) * 2 + core

    r = range(SIDE)
    plane = [[device(z, y, x, 0) for y in r for x in r] for z in r]
    plane += [[device(z, y, x, 1) for z in r for x in r] for y in r]
    long = {}
    for s in range(1, SIDE):
        long[s] = [
            pair
            for z in r
            for y in r
            for x in r
            for pair in (
                (device(z, y, x, 0), device((z + s) % SIDE, y, x, 0)),
                (device(z, y, x, 1), device(z, (y + s) % SIDE, x, 1)),
            )
        ]
    return plane, long


def lane_offset(lat_local):
    x = lax.axis_index("pos") % SIDE
    return (x % (HEAD_DIM // lat_local) * lat_local).astype(jnp.int32).reshape(1)


def rms_norm(values):
    return values * lax.rsqrt(jnp.mean(values * values, axis=-1, keepdims=True) + EPS)


def nt_dot(a, b):
    return lax.dot_general(a, b, (((1,), (1,)), ((), ())), preferred_element_type=F32)


def bf16_pieces(x):
    hi = x.astype(BF16).astype(F32)
    mid = (x - hi).astype(BF16).astype(F32)
    low = (x - hi - mid).astype(BF16).astype(F32)
    return hi, mid, low


def pack_rows(lse, heads):
    rows = jnp.concatenate([p[:heads] for p in bf16_pieces(lse)], axis=0)
    pad = jnp.zeros((LSE_ROWS - rows.shape[0], rows.shape[1]), F32)
    return jnp.concatenate([rows, pad], axis=0).astype(BF16)


def unpack_rows(packed, heads):
    x = packed.astype(F32)
    return x[:heads] + x[heads : 2 * heads] + x[2 * heads : 3 * heads]


def pipelined(count, score, use):
    score(0)
    for i in range(count):
        if i + 1 < count:
            score(i + 1)
        use(i)


def row_blocks(count, body):
    if count == 1:
        body(0)
    else:
        lax.fori_loop(0, count, lambda i, _: (body(i), 0)[1], 0)


def block_rows(i):
    start = i * ROW_BLOCK
    return pl.ds(start if isinstance(start, int) else pl.multiple_of(start, ROW_BLOCK), ROW_BLOCK)


def cross_kernel(valid_ref, q_ref, k_ref, v_ref, *refs, lat_local, first, heads, block_at, blocks):
    *before, out_ref, s_ref = refs
    rows = ROW_BLOCK
    owners = rows // lat_local
    all_heads = q_ref.shape[1] // HEAD_DIM
    done = first * lat_local
    span = done + heads * lat_local
    keys = k_ref.shape[0]
    valid = sum(valid_ref[i] for i in range(keys // BLK)) * BLK
    live = lax.broadcasted_iota(jnp.int32, (1, keys), 1) < valid
    bias = jnp.where(live, 0.0, MASKED)

    def block(step):
        lane = lax.broadcasted_iota(jnp.int32, (rows, HEAD_DIM), 1)
        mine_rows = block_rows(block_at + step)
        to = pl.ds(step * owners, owners)
        if before:
            out_ref[to, :done, :] = before[0][to, :done, :]
        stats = [jnp.zeros((rows, HEAD_DIM), F32), jnp.ones((rows, HEAD_DIM), F32)]

        def columns(i):
            return slice((first + i) * HEAD_DIM, (first + i + 1) * HEAD_DIM)

        def score(i):
            s_ref[i % 2] = nt_dot(q_ref[mine_rows, columns(i)], k_ref[:, columns(i)]) + bias

        def use(i):
            s = s_ref[i % 2]
            m = jnp.max(s, axis=1, keepdims=True)
            p = jnp.exp2((s - m) * (SCALE * LOG2E))
            total = jnp.sum(p, axis=1, keepdims=True)
            o = jnp.dot(p.astype(BF16), v_ref[:, columns(i)], preferred_element_type=F32)
            o = (o / total).astype(BF16)
            top = (first + i) * lat_local
            out_ref[to, top : top + lat_local, :] = o.reshape(owners, lat_local, HEAD_DIM)
            mine = lane % all_heads == first + i
            stats[0] = jnp.where(mine, m, stats[0])
            stats[1] = jnp.where(mine, total, stats[1])

        pipelined(heads, score, use)
        hi, mid, low = bf16_pieces(stats[0] * SCALE + jnp.log(stats[1]))
        place = lane // all_heads
        packed = jnp.where(place == 0, hi, jnp.where(place == 1, mid, jnp.where(place == 2, low, 0.0)))
        eye = lax.broadcasted_iota(jnp.int32, (LSE_ROWS, HEAD_DIM), 0)
        eye = (eye == lax.broadcasted_iota(jnp.int32, (LSE_ROWS, HEAD_DIM), 1)).astype(BF16)
        turned = nt_dot(eye, packed.astype(BF16)).astype(BF16)
        for d in range(owners):
            at = d * lat_local // HEAD_DIM * HEAD_DIM
            rows_d = turned[:, at : at + HEAD_DIM]
            if before:
                rows_d = rows_d + before[0][step * owners + d, done : done + LSE_ROWS, :]
            out_ref[step * owners + d, span : span + LSE_ROWS, :] = rows_d

    row_blocks(blocks, block)


def load_kernel(*refs):
    n = len(refs) // 2
    *pairs, sems = refs
    copies = [pltpu.make_async_copy(pairs[i], pairs[n + i], sems.at[i]) for i in range(n)]
    for copy in copies:
        copy.start()
    for copy in copies:
        copy.wait()


def join_kernel(*refs, lat_local):
    *parts, out_ref = refs
    owners, tall, _ = out_ref.shape
    span = tall - LSE_ROWS
    heads = span // lat_local
    group = HEAD_DIM // lat_local
    whole = [r for r in parts if r.shape[0] == owners]
    split = [r for r in parts if r.shape[0] != owners]
    for g in range(0, owners, group):
        parts = [(r, g) for r in whole]
        if split:
            parts.append((split[g // split[0].shape[0]], g % split[0].shape[0]))
        lses = [unpack_rows(r[at, span : span + LSE_ROWS, :], heads) for r, at in parts]
        top = functools.reduce(jnp.maximum, lses)
        ws = [jnp.exp(x - top) for x in lses]
        total = functools.reduce(jnp.add, ws)
        packed = pack_rows(top + jnp.log(total), heads)
        stacked = jnp.concatenate([w / total for w in ws], axis=0)
        wt = jnp.transpose(stacked)
        for d in range(group):
            out_ref[g + d, span : span + LSE_ROWS, :] = packed
            for h in range(heads):
                rows = slice(h * lat_local, (h + 1) * lat_local)
                acc = jnp.zeros((lat_local, HEAD_DIM), F32)
                for i, (r, at) in enumerate(parts):
                    w = wt[d * lat_local : (d + 1) * lat_local, i * heads + h : i * heads + h + 1]
                    acc = acc + w * r[at + d, rows, :].astype(F32)
                out_ref[g + d, rows, :] = acc.astype(BF16)


def combine_kernel(core_ref, r_ref, w_ref, mlp_ref, own_ref, other_ref, mlp_out, terms_ref, spot_ref, w_vmem, sems, *, lat_local):
    copies = [
        pltpu.make_async_copy(w_ref, w_vmem, sems.at[0]),
        pltpu.make_async_copy(mlp_ref, mlp_out, sems.at[1]),
    ]
    for copy in copies:
        copy.start()
    devices, tall, _ = r_ref.shape
    span = tall - LSE_ROWS
    heads = span // lat_local
    lses = [unpack_rows(r_ref[d, span : span + LSE_ROWS, :], heads) for d in range(devices)]
    top = functools.reduce(jnp.maximum, lses)
    ws = [jnp.exp(x - top) for x in lses]
    total = functools.reduce(jnp.add, ws)
    stacked = jnp.concatenate([w / total for w in ws], axis=0)
    spot_ref[...] = jnp.transpose(stacked)
    wt = spot_ref[pl.ds(pl.multiple_of(core_ref[1], lat_local), lat_local), :]
    parts = []
    for h in range(heads):
        acc = jnp.zeros((lat_local, HEAD_DIM), F32)
        for d in range(devices):
            w = wt[:, d * heads + h : d * heads + h + 1]
            acc = acc + w * r_ref[d, h * lat_local : (h + 1) * lat_local, :].astype(F32)
        parts.append(acc.astype(BF16))
    copies[0].wait()
    terms = jnp.zeros((lat_local, w_vmem.shape[1]), F32)
    for h in range(span // lat_local):
        terms = terms + jnp.dot(
            parts[h],
            w_vmem[h * HEAD_DIM : (h + 1) * HEAD_DIM, :],
            preferred_element_type=F32,
        )
    half = lat_local // 2
    terms_ref[...] = terms.reshape(2, half, w_vmem.shape[1])
    own_ref[...] = terms_ref[core_ref[0]]
    other_ref[...] = terms_ref[1 - core_ref[0]].astype(BF16)
    copies[1].wait()


def spread_kernel(l_ref, w_ref, out_ref, l_vmem, w_vmem, sems):
    copies = [
        pltpu.make_async_copy(w_ref, w_vmem, sems.at[0]),
        pltpu.make_async_copy(l_ref, l_vmem, sems.at[1]),
    ]
    for copy in copies:
        copy.start()
    for copy in copies:
        copy.wait()
    q = jnp.dot(l_vmem[...], w_vmem[...], preferred_element_type=F32).astype(BF16)
    out_ref[...] = jnp.broadcast_to(q[None], out_ref.shape)


def latent_kernel(own_ref, recv_ref, w_ref, out_ref):
    normed = rms_norm(own_ref[...] + recv_ref[...].astype(F32))
    hidden = jax.nn.gelu(jnp.dot(normed.astype(BF16), w_ref[...], preferred_element_type=F32))
    rows = (normed + hidden).astype(BF16)
    out_ref[...] = jnp.broadcast_to(rows[None], out_ref.shape)


def write_kv(row_refs, w_ref, out_ref, first):
    at = 0
    wide = w_ref.shape[1]
    for r in row_refs:
        n = r.shape[0]
        out_ref[at : at + n, first : first + wide] = jnp.dot(
            r[...], w_ref[...], preferred_element_type=F32
        ).astype(BF16)
        at += n


def kv_kernel(*refs):
    *row_refs, k_ref, v_ref, out_ref = refs
    write_kv(row_refs, k_ref, out_ref, 0)
    write_kv(row_refs, v_ref, out_ref, k_ref.shape[1])


def near_kv_kernel(near_ref, swapped_ref, k_ref, v_ref, p_ref, q_ref, out_ref, k_out, v_out, p_out, q_out, sems):
    pairs = ((k_ref, k_out), (v_ref, v_out), (p_ref, p_out), (q_ref, q_out))
    copies = [pltpu.make_async_copy(a, b, sems.at[i]) for i, (a, b) in enumerate(pairs)]
    for copy in copies:
        copy.start()
    rows = (near_ref, swapped_ref)
    copies[0].wait()
    write_kv(rows, k_out, out_ref, 0)
    copies[1].wait()
    write_kv(rows, v_out, out_ref, k_out.shape[1])
    copies[2].wait()
    copies[3].wait()


def head_columns(columns, h):
    return (
        slice(h * HEAD_DIM, (h + 1) * HEAD_DIM),
        slice(columns + h * HEAD_DIM, columns + (h + 1) * HEAD_DIM),
    )


def near_kernel(q_ref, kv_ref, sums_ref, tops_ref, totals_ref, s_ref):
    columns = q_ref.shape[1]
    shape = (ROW_BLOCK, HEAD_DIM)

    def block(step):
        rows = block_rows(step)

        def score(h):
            kc, _ = head_columns(columns, h)
            s_ref[h % 2] = nt_dot(q_ref[rows, kc], kv_ref[:, kc])

        def use(h):
            kc, vc = head_columns(columns, h)
            s = s_ref[h % 2]
            m = jnp.max(s, axis=1, keepdims=True)
            p = jnp.exp2((s - m) * (SCALE * LOG2E))
            sums_ref[rows, kc] = jnp.dot(p.astype(BF16), kv_ref[:, vc], preferred_element_type=F32)
            tops_ref[rows, kc] = jnp.broadcast_to(m, shape)
            totals_ref[rows, kc] = jnp.broadcast_to(jnp.sum(p, axis=1, keepdims=True), shape)

        pipelined(columns // HEAD_DIM, score, use)

    row_blocks(q_ref.shape[0] // ROW_BLOCK, block)


def attend(rows, q_ref, carried_refs, kv_refs, w_ref, s_ref, o_ref):
    sums_ref, tops_ref, totals_ref = carried_refs
    columns = q_ref.shape[1]
    spots = []
    at = 0
    for kv in kv_refs:
        spots.append(slice(at, at + kv.shape[0]))
        at += kv.shape[0]

    def score(h):
        kc, _ = head_columns(columns, h)
        for spot, kv in zip(spots, kv_refs):
            s_ref[h % 2, :, spot] = nt_dot(q_ref[rows, kc], kv[:, kc])

    def use(h):
        kc, vc = head_columns(columns, h)
        s = s_ref[h % 2]
        before = tops_ref[rows, kc]
        m = jnp.maximum(before, jnp.max(s, axis=1, keepdims=True))
        keep = jnp.exp2((before - m) * (SCALE * LOG2E))
        p = jnp.exp2((s - m[:, :1]) * (SCALE * LOG2E))
        total = totals_ref[rows, kc] * keep + jnp.sum(p, axis=1, keepdims=True)
        o = sums_ref[rows, kc] * keep
        pb = p.astype(BF16)
        for spot, kv in zip(spots, kv_refs):
            o = o + jnp.dot(pb[:, spot], kv[:, vc], preferred_element_type=F32)
        o_ref[:, kc] = (o / total).astype(BF16)

    pipelined(columns // HEAD_DIM, score, use)
    return jnp.dot(o_ref[...], w_ref[...], preferred_element_type=F32)


def decode_kernel(base_ref, q_ref, *refs):
    carried, (*kv_refs, w_ref, out_ref, s_ref, o_ref) = refs[:3], refs[3:]

    def block(step):
        rows = block_rows(base_ref[0] + step)
        terms = attend(rows, q_ref, carried, kv_refs, w_ref, s_ref, o_ref)
        out_ref[block_rows(step), :] = terms.astype(out_ref.dtype)

    row_blocks(out_ref.shape[0] // ROW_BLOCK, block)


def last_kernel(base_ref, q_ref, *refs):
    carried, (*kv_refs, w_ref, first_ref, recv_ref, out_ref, s_ref, o_ref, out_vmem, sems) = refs[:3], refs[3:]
    n = first_ref.shape[0]

    def leave(i, rows, terms):
        out_vmem[rows, :] = rms_norm(terms + recv_ref[rows, :].astype(F32)).astype(BF16)
        copy = pltpu.make_async_copy(out_vmem.at[rows, :], out_ref.at[rows, :], sems.at[i])
        copy.start()
        return copy

    early = leave(0, pl.ds(0, n), first_ref[...])
    terms = attend(block_rows(base_ref[0]), q_ref, carried, kv_refs, w_ref, s_ref, o_ref)
    late = leave(1, pl.ds(n, ROW_BLOCK), terms)
    early.wait()
    late.wait()


def params(limit=56 << 20):
    return pltpu.CompilerParams(vmem_limit_bytes=limit)


def cross(valid, q, k, v, lat_local, first, heads, before=None, block_at=0, blocks=None):
    blocks = q.shape[0] // ROW_BLOCK if blocks is None else blocks
    lat = blocks * ROW_BLOCK
    tall = (first + heads) * lat_local + LSE_ROWS
    extra = () if before is None else (before,)
    vmem = pl.BlockSpec(memory_space=pltpu.VMEM)
    return pl.pallas_call(
        functools.partial(
            cross_kernel, lat_local=lat_local, first=first, heads=heads, block_at=block_at, blocks=blocks
        ),
        out_shape=jax.ShapeDtypeStruct((lat // lat_local, tall, HEAD_DIM), BF16),
        in_specs=[pl.BlockSpec(memory_space=pltpu.SMEM)] + [vmem] * (3 + len(extra)),
        out_specs=vmem,
        scratch_shapes=[pltpu.VMEM((2, ROW_BLOCK, k.shape[0]), F32)],
        compiler_params=params(32 << 20),
        cost_estimate=pl.CostEstimate(
            flops=4 * lat * k.shape[0] * heads * HEAD_DIM,
            bytes_accessed=4 << 20,
            transcendentals=lat * k.shape[0] * heads,
        ),
        name="cross",
    )(valid, q, k, v, *extra)


def in_hbm(*arrays):
    return [pltpu.with_memory_space_constraint(x, pltpu.HBM) for x in arrays]


def load(arrays):
    return pl.pallas_call(
        load_kernel,
        out_shape=[jax.ShapeDtypeStruct(x.shape, x.dtype) for x in arrays],
        in_specs=[pl.BlockSpec(memory_space=pltpu.HBM)] * len(arrays),
        out_specs=[pl.BlockSpec(memory_space=pltpu.VMEM)] * len(arrays),
        scratch_shapes=[pltpu.SemaphoreType.DMA((len(arrays),))],
        compiler_params=params(8 << 20),
        name="load",
    )(*in_hbm(*arrays))


def join(parts, lat_local):
    vmem = pl.BlockSpec(memory_space=pltpu.VMEM)
    return pl.pallas_call(
        functools.partial(join_kernel, lat_local=lat_local),
        out_shape=jax.ShapeDtypeStruct(parts[0].shape, BF16),
        in_specs=[vmem] * len(parts),
        out_specs=vmem,
        compiler_params=params(24 << 20),
        name="join",
    )(*parts)


def combine(core, gathered, w_out, w_mlp, lat_local):
    width = w_out.shape[1]
    half = lat_local // 2
    vmem = pl.BlockSpec(memory_space=pltpu.VMEM)
    hbm = pl.BlockSpec(memory_space=pltpu.HBM)
    return pl.pallas_call(
        functools.partial(combine_kernel, lat_local=lat_local),
        out_shape=(
            jax.ShapeDtypeStruct((half, width), F32),
            jax.ShapeDtypeStruct((half, width), BF16),
            jax.ShapeDtypeStruct(w_mlp.shape, BF16),
        ),
        in_specs=[pl.BlockSpec(memory_space=pltpu.SMEM), vmem, hbm, hbm],
        out_specs=(vmem, vmem, vmem),
        scratch_shapes=[
            pltpu.VMEM((2, half, width), F32),
            pltpu.VMEM((HEAD_DIM, gathered.shape[0] * (w_out.shape[0] // HEAD_DIM)), F32),
            pltpu.VMEM(w_out.shape, BF16),
            pltpu.SemaphoreType.DMA((2,)),
        ],
        compiler_params=params(24 << 20),
        name="combine",
    )(core, gathered, *in_hbm(w_out, w_mlp))


def spread(latents, w_query, devices):
    hbm = pl.BlockSpec(memory_space=pltpu.HBM)
    return pl.pallas_call(
        spread_kernel,
        out_shape=jax.ShapeDtypeStruct((devices, latents.shape[0], w_query.shape[1]), BF16),
        in_specs=[hbm, hbm],
        out_specs=pl.BlockSpec(memory_space=pltpu.VMEM),
        scratch_shapes=[
            pltpu.VMEM(latents.shape, BF16),
            pltpu.VMEM(w_query.shape, BF16),
            pltpu.SemaphoreType.DMA((2,)),
        ],
        compiler_params=params(60 << 20),
        name="spread",
    )(*in_hbm(latents, w_query))


def latent_rows(own, recv, w_mlp, devices):
    vmem = pl.BlockSpec(memory_space=pltpu.VMEM)
    return pl.pallas_call(
        latent_kernel,
        out_shape=jax.ShapeDtypeStruct((devices,) + own.shape, BF16),
        in_specs=[vmem] * 3,
        out_specs=vmem,
        compiler_params=params(24 << 20),
        name="latent",
    )(own, recv, w_mlp)


def latent_kv(rows, w_lkey, w_lvalue):
    vmem = pl.BlockSpec(memory_space=pltpu.VMEM)
    total = sum(r.shape[0] for r in rows)
    wide = w_lkey.shape[1] * 2
    return pl.pallas_call(
        kv_kernel,
        out_shape=jax.ShapeDtypeStruct((total, wide), BF16),
        in_specs=[vmem] * (len(rows) + 2),
        out_specs=vmem,
        compiler_params=params(24 << 20),
        cost_estimate=pl.CostEstimate(
            flops=2 * total * wide * w_lkey.shape[0], bytes_accessed=4 << 20, transcendentals=0
        ),
        name="latent_kv",
    )(*rows, w_lkey, w_lvalue)


def near_kv(near, swapped, w_lkey, w_lvalue, w_pout, queries):
    vmem = pl.BlockSpec(memory_space=pltpu.VMEM)
    hbm = pl.BlockSpec(memory_space=pltpu.HBM)
    rows = near.shape[0] + swapped.shape[0]
    return pl.pallas_call(
        near_kv_kernel,
        out_shape=[
            jax.ShapeDtypeStruct((rows, 2 * w_lkey.shape[1]), BF16),
            *[jax.ShapeDtypeStruct(w.shape, BF16) for w in (w_lkey, w_lvalue, w_pout, queries)],
        ],
        in_specs=[vmem, vmem, hbm, hbm, hbm, hbm],
        out_specs=[vmem] * 5,
        scratch_shapes=[pltpu.SemaphoreType.DMA((4,))],
        compiler_params=params(24 << 20),
        cost_estimate=pl.CostEstimate(
            flops=4 * rows * w_lkey.size // 2, bytes_accessed=4 << 20, transcendentals=0
        ),
        name="near_kv",
    )(near, swapped, *in_hbm(w_lkey, w_lvalue, w_pout, queries))


def near_decode(q, kv):
    rows, columns = q.shape
    vmem = pl.BlockSpec(memory_space=pltpu.VMEM)
    return pl.pallas_call(
        near_kernel,
        out_shape=(jax.ShapeDtypeStruct((rows, columns), F32),) * 3,
        in_specs=[vmem] * 2,
        out_specs=(vmem,) * 3,
        scratch_shapes=[pltpu.VMEM((2, ROW_BLOCK, kv.shape[0]), F32)],
        compiler_params=params(24 << 20),
        cost_estimate=pl.CostEstimate(
            flops=4 * rows * columns * kv.shape[0], bytes_accessed=4 << 20, transcendentals=4 * rows * kv.shape[0]
        ),
        name="near_decode",
    )(q, kv)


def decode(base, blocks, q, carried, kvs, w_pout, dtype, finish=()):
    columns = q.shape[1]
    width = w_pout.shape[1]
    rows = blocks * ROW_BLOCK
    out_rows = finish[1].shape[0] if finish else rows
    keys = sum(kv.shape[0] for kv in kvs)
    vmem = pl.BlockSpec(memory_space=pltpu.VMEM)
    scratch = [pltpu.VMEM((2, ROW_BLOCK, keys), F32), pltpu.VMEM((ROW_BLOCK, columns), BF16)]
    if finish:
        scratch += [pltpu.VMEM((out_rows, width), BF16), pltpu.SemaphoreType.DMA((2,))]
    operands = (q, *carried, *kvs, w_pout, *finish)
    return pl.pallas_call(
        last_kernel if finish else decode_kernel,
        out_shape=jax.ShapeDtypeStruct((out_rows, width), dtype),
        in_specs=[pl.BlockSpec(memory_space=pltpu.SMEM)] + [vmem] * len(operands),
        out_specs=pl.BlockSpec(memory_space=pltpu.HBM) if finish else vmem,
        scratch_shapes=scratch,
        compiler_params=params(30 << 20),
        cost_estimate=pl.CostEstimate(
            flops=4 * rows * columns * keys, bytes_accessed=8 << 20, transcendentals=4 * rows * keys
        ),
        name="decode",
    )(base, *operands)


def project(a, w):
    return jnp.dot(a, w, preferred_element_type=F32).astype(BF16)


def per_device(
    inputs,
    valid_blocks,
    latents,
    w_query,
    w_key,
    w_value,
    w_out,
    w_mlp,
    w_lkey,
    w_lvalue,
    w_pquery,
    w_pout,
):
    lat_local = latents.shape[0]
    columns = w_key.shape[1]
    width = inputs.shape[1]
    core = lax.axis_index("head").astype(jnp.int32).reshape(1)
    swap = [(0, 1), (1, 0)]

    plane, long = plane_groups()

    def within_plane(x):
        return lax.all_to_all(x, AXES, 0, 0, axis_index_groups=plane)

    def along(x, shift):
        return lax.ppermute(x, AXES, long[shift % SIDE])

    queries = within_plane(spread(latents, w_query, SIDE * SIDE)).reshape(-1, columns)
    keys = project(inputs, w_key)
    values = project(inputs, w_value)
    places = jnp.concatenate([core, lane_offset(lat_local)])
    queries, keys, values, places = lax.optimization_barrier((queries, keys, values, places))
    away = [along(queries, s) for s in ORDER]
    keys, values = load((keys, values))
    heads = columns // HEAD_DIM
    half = cross(valid_blocks, queries, keys, values, lat_local, 0, heads // 2)
    part, partials = half, []
    *soon, final = ORDER
    for s, there in zip(soon, away):
        part, there = lax.optimization_barrier((part, there))
        part = cross(valid_blocks, there, keys, values, lat_local, 0, heads)
        partials.append(along(part, -s))
    there, late = away[-1], []
    for i in range(2):
        part, there = lax.optimization_barrier((part, there))
        part = cross(valid_blocks, there, keys, values, lat_local, 0, heads, None, i, 1)
        late.append(along(part, -final))
    part, half, inputs = lax.optimization_barrier((part, half, inputs))
    stay = cross(valid_blocks, queries, keys, values, lat_local, heads // 2, heads // 2, half)
    pos_queries = project(inputs, w_pquery)
    stay, pos_queries, late = lax.optimization_barrier((join([stay, *partials], lat_local), pos_queries, late))
    partials = [stay, *late]
    gathered = within_plane(join(partials, lat_local))
    own, other, w_mlp = combine(places, gathered, w_out, w_mlp, lat_local)
    recv = lax.ppermute(other, "head", swap)
    rows = latent_rows(own, recv, w_mlp, SIDE * SIDE)
    near = within_plane(rows)
    near = near.reshape(-1, width)
    far = []
    for s in FAR_ORDER:
        far.append(along(near, s))
    near_swapped = lax.ppermute(near, "head", swap)
    kv, w_lkey, w_lvalue, w_pout, pos_queries = near_kv(
        near, near_swapped, w_lkey, w_lvalue, w_pout, pos_queries
    )
    carried = near_decode(pos_queries, kv)
    slow, *quick = far
    carried, quick = lax.optimization_barrier((carried, quick))
    quick_swapped = [lax.ppermute(x, "head", swap) for x in quick]
    quick_kv = latent_kv(quick, w_lkey, w_lvalue)
    slow, quick_kv = lax.optimization_barrier((slow, quick_kv))
    slow_swapped = lax.ppermute(slow, "head", swap)
    swapped_kv = latent_kv(quick_swapped, w_lkey, w_lvalue)
    slow_kv = latent_kv([slow, slow_swapped], w_lkey, w_lvalue)
    kvs = [quick_kv, swapped_kv, slow_kv]
    blocks = pos_queries.shape[0] // 2 // ROW_BLOCK
    terms = decode((1 - core) * blocks, blocks, pos_queries, carried, kvs, w_pout, BF16)
    arrived = lax.ppermute(terms, "head", swap)
    first = decode(core * blocks, blocks - 1, pos_queries, carried, kvs, w_pout, F32)
    return decode(core * blocks + blocks - 1, 1, pos_queries, carried, kvs, w_pout, BF16, (first, arrived))


def solution(mesh):
    placed = (
        P("pos", None),
        P("pos"),
        P("pos", None),
        P(None, "head"),
        P(None, "head"),
        P(None, "head"),
        P("head", None),
        P(),
        P(None, "head"),
        P(None, "head"),
        P(None, "head"),
        P("head", None),
    )

    return jax.shard_map(
        per_device,
        mesh=mesh,
        in_specs=placed,
        out_specs=P(("pos", "head"), None),
        check_vma=False,
    )
```
